256 devices in a mesh: space: 32 (over x, z_hi, y), vel: 8 (over z_lo, core).
Axes of the slice: x: 4, y: 4, z: 8 (z_hi: 2, z_lo: 4; z = z_hi * 4 + z_lo), core: 2. Of those that a mesh axis runs over, the one named last changes fastest.
Arguments:
- distribution: float32 [64, 128, 4096], P('space', None, 'vel'), may hold values from 0.05 to 1
- cell_flags: int32 [64, 128], P('space'), may hold values from 0 to 3, as said below
- kernel_alpha: float32 [8, 4096], replicated, may hold values from -1 to 1, as said below
- kernel_beta: float32 [8, 4096], replicated, may hold values from -1 to 1, as said below
- kernel_loss: float32 [4096], replicated, may hold values from 0 to 1, as said below
- boundary_states: float32 [2, 4096], replicated, may hold values from 0.05 to 1
Outputs:
- updated: float32 [64, 128, 4096], P('space', None, 'vel')
The draws below stay inside these ranges and needn't reach their ends.
Inputs may be any that keep to these rules, and one draw needn't show every extreme that they name: `cell_flags`: 0 marks a fluid cell, 1 a wall cell, 2 an inflow cell, 3 an outflow cell; every type occurs. `kernel_alpha`: even in the mode: the entry of mode (k1, k2, k3) equals that of mode (-k1, -k2, -k3) modulo 16, for every direction. `kernel_beta`: even in the mode, as kernel_alpha. `kernel_loss`: even in the mode, as kernel_alpha.
All inputs are finite; a program needn't handle non-finite values.
Results may differ from the reference program's by a relative error of at most 0.0001.
Values sent between devices are 32-bit elements; how exact they have to be, the bound alone decides.
A program may use at most 64 MiB of HBM per device.

```python
import math
from functools import partial
import jax
import jax.numpy as jnp
from jax import lax

VG = 16
DIRS = 8
CS = 128
VEL = 4096
NX = 64


def even_modes(raw_modes):
    flipped = jnp.roll(jnp.flip(raw_modes, axis=(1, 2, 3)), 1, axis=(1, 2, 3))
    return 0.5 * (raw_modes + flipped)


def signed_modes(key, count):
    raw_modes = jax.random.uniform(key, (count, VG, VG, VG), jnp.float32, -1.0, 1.0)
    return even_modes(raw_modes).reshape(count, VEL)


def draw_cell_flags(key, part):
    levels = jax.random.randint(jax.random.fold_in(key, 11), (NX, CS), 0, 8)
    return jnp.where(levels < 5, 0, levels - 4).astype(jnp.int32)


def draw_kernel_alpha(key, part):
    return signed_modes(jax.random.fold_in(key, 21), DIRS)


def draw_kernel_beta(key, part):
    return signed_modes(jax.random.fold_in(key, 31), DIRS)


def draw_kernel_loss(key, part):
    raw_modes = jax.random.uniform(jax.random.fold_in(key, 41), (1, VG, VG, VG), jnp.float32, 0.0, 1.0)
    return even_modes(raw_modes).reshape(VEL)


def block_scale(stream_key, shape, cuts, least, top_value):
    gain, own = 1.0, jax.random.fold_in(stream_key, 6)
    for axis_at, shards_of in cuts:
        steps = jnp.exp(jax.random.uniform(jax.random.fold_in(own, axis_at), (shards_of,), jnp.float32, least / len(cuts), top_value / len(cuts)))
        gain = gain * jnp.repeat(steps, shape[axis_at] // shards_of).reshape([-1 if axis == axis_at else 1 for axis in range(len(shape))])
    return gain


def setup_inputs(seed: int = 0) -> dict:
    keys = jax.random.split(jax.random.key(seed), 7)
    distribution = jnp.clip(jnp.exp(math.log(1.0) - 2.9957323 * jax.random.uniform(keys[0], (NX, CS, VEL), jnp.float32) ** block_scale(keys[0], (NX, CS, VEL), ((0, 32), (2, 8)), -0.2, 0.2)), 0.05, 1.0)
    cell_flags = draw_cell_flags(jax.random.fold_in(keys[6], 71), 0)
    kernel_alpha = draw_kernel_alpha(jax.random.fold_in(keys[6], 71), 0)
    kernel_beta = draw_kernel_beta(jax.random.fold_in(keys[6], 71), 0)
    kernel_loss = draw_kernel_loss(jax.random.fold_in(keys[6], 71), 0)
    boundary_states = jnp.clip(jnp.exp(jax.random.uniform(keys[5], (2, VEL), jnp.float32, math.log(0.05), math.log(1.0))), 0.05, 1.0)
    return {"distribution": distribution, "cell_flags": cell_flags, "kernel_alpha": kernel_alpha, "kernel_beta": kernel_beta, "kernel_loss": kernel_loss, "boundary_states": boundary_states}


courant_max = 0.9
collision_step = 0.5


def courant(vel_ids):
    slow_index = vel_ids // (VG * VG)
    return courant_max * (2.0 * slow_index.astype(jnp.float32) + 1.0 - VG) / (VG - 1.0)


def ghosted(state_in, cell_flags, boundary_states):
    cell_marks = cell_flags[:, :, None]
    return jnp.where(cell_marks == 1, boundary_states[0], jnp.where(cell_marks == 2, boundary_states[1], state_in))


def stencil(ghost_vals, up_one, up_two, abs_rate, cell_flags):
    second = ghost_vals - 0.5 * abs_rate * (3.0 * ghost_vals - 4.0 * up_one + up_two) + 0.5 * abs_rate * abs_rate * (ghost_vals - 2.0 * up_one + up_two)
    first_order = ghost_vals - abs_rate * (ghost_vals - up_one)
    cell_marks = cell_flags[:, :, None]
    return jnp.where(cell_marks == 0, second, jnp.where(cell_marks == 3, first_order, ghost_vals))


def half_transport(state_in, cell_flags, boundary_states):
    ghost_vals = ghosted(state_in, cell_flags, boundary_states)
    courant_num = courant(jnp.arange(VEL, dtype=jnp.int32))
    positive = courant_num > 0
    cell_count = ghost_vals.shape[0]
    padded = jnp.pad(ghost_vals, ((2, 2), (0, 0), (0, 0)))
    up_one = jnp.where(positive, padded[1:cell_count + 1], padded[3:cell_count + 3])
    up_two = jnp.where(positive, padded[0:cell_count], padded[4:cell_count + 4])
    return stencil(ghost_vals, up_one, up_two, jnp.abs(courant_num), cell_flags)


def collide_block(kernel_alpha, kernel_beta, kernel_loss, cell_block):
    cell_count = cell_block.shape[0]
    cell_cube = cell_block.reshape(cell_count, VG, VG, VG)
    spectrum = jnp.fft.fftn(cell_cube, axes=(1, 2, 3))
    alpha_modes = kernel_alpha.reshape(-1, VG, VG, VG)
    beta_modes = kernel_beta.reshape(-1, VG, VG, VG)
    gain_sum = jnp.zeros_like(cell_cube)
    for direction in range(alpha_modes.shape[0]):
        first_part = jnp.fft.ifftn(alpha_modes[direction] * spectrum, axes=(1, 2, 3)).real
        second_part = jnp.fft.ifftn(beta_modes[direction] * spectrum, axes=(1, 2, 3)).real
        gain_sum = gain_sum + first_part * second_part
    loss_part = jnp.fft.ifftn(kernel_loss.reshape(VG, VG, VG) * spectrum, axes=(1, 2, 3)).real
    result = cell_cube + collision_step * (gain_sum - cell_cube * loss_part)
    return result.reshape(cell_count, VEL)


def reference(distribution, cell_flags, kernel_alpha, kernel_beta, kernel_loss, boundary_states):
    moved_half = half_transport(distribution, cell_flags, boundary_states)
    total_cells = NX * CS
    block_size = math.gcd(total_cells, 256)
    blocks = moved_half.reshape(total_cells // block_size, block_size, VEL)
    collided = lax.map(partial(collide_block, kernel_alpha, kernel_beta, kernel_loss), blocks)
    collided = collided.reshape(NX, CS, VEL)
    return half_transport(collided, cell_flags, boundary_states)
```

```python
import functools

import jax
import jax.numpy as jnp
import numpy as np
from jax import lax
from jax.experimental import pallas as pl
from jax.experimental.pallas import tpu as pltpu
from jax.sharding import PartitionSpec as P

VG = 16
PLANE = VG * VG
VEL = VG * PLANE
DIRS = 8
FILTERS = 2 * DIRS + 1
PEERS = 8
SLAB = 16
ROWS = 8
CHUNKS = SLAB // ROWS
COLUMN = 4
MESH = pl.DeviceIdType.MESH
f32 = jnp.float32
bf16 = jnp.bfloat16


def half_modes():
    own = [((0, 0), (0, 8)), ((8, 0), (8, 8))]
    seen, pairs = set(), []
    for a in range(VG):
        for b in range(VG):
            twin = ((-a) % VG, (-b) % VG)
            if twin == (a, b) or twin in seen:
                continue
            seen.add((a, b))
            pairs.append((a, b))
    return own, pairs


def tables():
    own, pairs = half_modes()
    j, l = np.meshgrid(np.arange(VG), np.arange(VG), indexing="ij")
    j, l = j.reshape(-1), l.reshape(-1)

    def angle(mode):
        return ((mode[0] * j + mode[1] * l) % VG) * (2.0 * np.pi / VG)

    forward = np.zeros((PLANE, PLANE))
    inverse = np.zeros((PLANE, PLANE))
    pick = np.zeros((PLANE, PLANE))
    half = PLANE // 2
    for lane, (first, second) in enumerate(own):
        forward[:, lane] = np.cos(angle(first))
        forward[:, half + lane] = np.cos(angle(second))
        inverse[lane] = np.cos(angle(first))
        inverse[half + lane] = np.cos(angle(second))
        one, two = (first[0] * VG + first[1], second[0] * VG + second[1])
        pick[one, lane] = pick[two, lane] = 0.5
        pick[one, half + lane], pick[two, half + lane] = 0.5, -0.5
    for lane, mode in enumerate(pairs, start=len(own)):
        forward[:, lane] = np.cos(angle(mode))
        forward[:, half + lane] = -np.sin(angle(mode))
        inverse[lane] = 2.0 * np.cos(angle(mode))
        inverse[half + lane] = -2.0 * np.sin(angle(mode))
        pick[mode[0] * VG + mode[1], lane] = 1.0

    def parts(table):
        high = table.astype(np.float32).astype(bf16)
        low = (table - high.astype(np.float64)).astype(np.float32).astype(bf16)
        return [high, low]

    stack = parts(forward) + parts(inverse / VEL) + [pick.astype(bf16)]
    return np.stack(stack)


def times_root(re, im, power):
    power %= VG
    if power == 0:
        return re, im
    if power == 4:
        return im, -re
    c = float(np.cos(2.0 * np.pi * power / VG))
    s = float(np.sin(2.0 * np.pi * power / VG))
    if power == 2:
        return (re + im) * c, (im - re) * c
    if power == 6:
        return (im - re) * s, (re + im) * (-s)
    return re * c + im * s, im * c - re * s


def four_points(z):
    (ar, ai), (br, bi), (cr, ci), (dr, di) = z
    pr, pi_, mr, mi = ar + cr, ai + ci, ar - cr, ai - ci
    qr, qi, nr, ni = br + dr, bi + di, br - dr, bi - di
    return [(pr + qr, pi_ + qi), (mr + ni, mi - nr), (pr - qr, pi_ - qi), (mr - ni, mi + nr)]


def line_transform(z):
    mid = [four_points([z[4 * a + b] for a in range(4)]) for b in range(4)]
    out = [None] * VG
    for k in range(4):
        group = four_points([times_root(*mid[b][k], b * k) for b in range(4)])
        for m in range(4):
            out[k + 4 * m] = group[m]
    return out


def line_inverse(z):
    flipped = line_transform([(im, re) for re, im in z])
    return [(re, im) for im, re in flipped]


def split_two(x):
    high = x.astype(bf16)
    return high, (x - high.astype(f32)).astype(bf16)


def dot_three(x, high, low):
    x_high, x_low = split_two(x)
    dot = functools.partial(jnp.dot, preferred_element_type=f32)
    return dot(x_high, high) + (dot(x_low, high) + dot(x_high, low))


def flag_column(row, offset):
    lanes = lax.broadcasted_iota(jnp.int32, (ROWS, 128), 1)
    rows = lax.broadcasted_iota(jnp.int32, (ROWS, 128), 0)
    wide = jnp.broadcast_to(row.astype(f32), (ROWS, 128))
    return jnp.sum(jnp.where(lanes == rows + offset, wide, 0.0), axis=1, keepdims=True)


def transport(flags, states, own_ref, left_ref, right_ref, put):
    left, own, right = flags[0:2], flags[2:4], flags[4:6]

    def ghost(val, mark, low, high, edge):
        if edge:
            val = jnp.where(mark == 4.0, 0.0, val)
        return jnp.where(mark == 1.0, low, jnp.where(mark == 2.0, high, val))

    def stencil(g, one, two, a, mark):
        second = (1.0 - 1.5 * a + 0.5 * a * a) * g + (2.0 * a - a * a) * one + (0.5 * a * a - 0.5 * a) * two
        return jnp.where(mark == 0.0, second, jnp.where(mark == 3.0, g - a * (g - one), g))

    def side(v, positive):
        for part in range(2):
            lanes = slice(part * PLANE, (part + 1) * PLANE)
            a = jnp.abs((2 * (2 * v + part) - 15).astype(f32)) * (0.9 / 15.0)
            low, high = states[v, 0, part : part + 1, :], states[v, 1, part : part + 1, :]
            own0 = ghost(own_ref[v, 0, :, lanes], own[0], low, high, False)
            own1 = ghost(own_ref[v, 1, :, lanes], own[1], low, high, False)
            if positive:
                near = ghost(left_ref[v - 4, 1, :, lanes], left[1], low, high, True)
                far = ghost(left_ref[v - 4, 0, :, lanes], left[0], low, high, True)
                put(v, part, stencil(own0, near, far, a, own[0]), stencil(own1, own0, near, a, own[1]))
            else:
                near = ghost(right_ref[v, 0, :, lanes], right[0], low, high, True)
                far = ghost(right_ref[v, 1, :, lanes], right[1], low, high, True)
                put(v, part, stencil(own0, own1, near, a, own[0]), stencil(own1, near, far, a, own[1]))

    @pl.loop(0, 4)
    def _(v):
        side(v, False)

    @pl.loop(4, 8)
    def _(v):
        side(v, True)


def collide(filters, tab, moved, spec, modes, first, second, gain):
    rows = VG * 2 * ROWS
    half = PLANE // 2

    def piece(ref, k, x):
        at = k * 2 * ROWS + x * ROWS
        return ref[at : at + ROWS, 0:half], ref[at : at + ROWS, half:PLANE]

    def put(ref, k, x, val):
        at = k * 2 * ROWS + x * ROWS
        ref[at : at + ROWS, 0:half] = val[0]
        ref[at : at + ROWS, half:PLANE] = val[1]

    spec[...] = dot_three(moved[...], tab[0], tab[1])
    for x in range(2):
        done = line_transform([piece(spec, k, x) for k in range(VG)])
        for k in range(VG):
            put(modes, k, x, done[k])

    def filtered(index, target):
        for x in range(2):
            z = [piece(modes, k, x) for k in range(VG)]
            w = []
            for k in range(VG):
                near, far = filters[index, k, 0], filters[index, k, 1]
                twin = z[-k % VG]
                w.append((near * z[k][0] + far * twin[0], near * z[k][1] - far * twin[1]))
            done = line_inverse(w)
            for k in range(VG):
                put(target, k, x, done[k])

    filtered(2 * DIRS, first)
    loss = dot_three(first[...], tab[2], tab[3])
    gain[...] = -(moved[...] * loss)

    @pl.loop(0, DIRS)
    def _(p):
        filtered(p, first)
        filtered(p + DIRS, second)
        one = dot_three(first[...], tab[2], tab[3])
        two = dot_three(second[...], tab[2], tab[3])
        gain[...] += one * two


def step_kernel(
    column, dist, flags, alpha, beta, loss, states, tab, out,
    recv, left1, right1, coll, left2, right2, done, moved, spec, modes, first, second, gain,
    packed, filters, near_flags, marks,
    in_send, in_recv, out_send, out_recv, halo_send, halo_recv, flag_send, flag_recv,
):
    s, v = lax.axis_index("space"), lax.axis_index("vel")
    total = lax.axis_size("space")

    def upper(at):
        return (at // column) % 2

    def slab_of(at, peer):
        turned = (3 - peer // 2) * 2 + peer % 2
        return peer + upper(at) * (turned - peer)

    def partner(at):
        turned = (3 - v // 2) * 2 + v % 2
        change = (upper(at) + upper(s)) % 2
        return {"space": at, "vel": v + change * (turned - v)}

    right = partner((s + 1) % total)
    left = partner((s + total - 1) % total)
    peers = [(v + d) % PEERS for d in range(1, PEERS)]

    barrier = pltpu.get_barrier_semaphore()
    for w in peers:
        pl.semaphore_signal(barrier, inc=1, device_id={"space": s, "vel": w}, device_id_type=MESH)
    for at in (left, right):
        pl.semaphore_signal(barrier, inc=1, device_id=at, device_id_type=MESH)
    pl.semaphore_wait(barrier, PEERS + 1)

    def remote(src, dst, send, rec, at):
        return pltpu.make_async_remote_copy(
            src_ref=src, dst_ref=dst, send_sem=send, recv_sem=rec, device_id=at, device_id_type=MESH
        )

    def cells(peer, n):
        return pl.ds(pl.multiple_of(slab_of(s, peer) * SLAB + n * ROWS, ROWS), ROWS)

    sent = []
    to_right = remote(flags, near_flags.at[0], flag_send.at[0], flag_recv.at[0], right)
    to_left = remote(flags, near_flags.at[1], flag_send.at[1], flag_recv.at[1], left)
    to_right.start()
    to_left.start()
    for n in range(CHUNKS):
        for d, w in enumerate(peers):
            copy = remote(dist.at[:, cells(w, n), :], recv.at[n, v], in_send.at[n, d], in_recv.at[n, v], {"space": s, "vel": w})
            copy.start()
            sent.append(copy)
        pltpu.make_async_copy(dist.at[:, cells(v, n), :], recv.at[n, v], in_recv.at[n, v]).start()

    for which, ref in enumerate((alpha, beta)):
        table = jnp.concatenate([ref[:, k * PLANE : (k + 1) * PLANE] for k in range(VG)], 0)
        one, rest = table.astype(bf16), table
        total_rows = jnp.zeros((VG * DIRS, PLANE), f32)
        for _ in range(3):
            one = rest.astype(bf16)
            rest = rest - one.astype(f32)
            total_rows = total_rows + jnp.dot(one, tab[4], preferred_element_type=f32)
        packed[which * VG * DIRS : (which + 1) * VG * DIRS, :] = total_rows
    rest = loss[...]
    total_rows = jnp.zeros((VG, PLANE), f32)
    for _ in range(3):
        one = rest.astype(bf16)
        rest = rest - one.astype(f32)
        total_rows = total_rows + jnp.dot(one, tab[4], preferred_element_type=f32)
    packed[2 * VG * DIRS :, :] = total_rows
    for k in range(VG):
        for f in range(FILTERS):
            at = 2 * VG * DIRS + k if f == 2 * DIRS else (f // DIRS) * VG * DIRS + k * DIRS + f % DIRS
            for part in range(2):
                row = packed[at : at + 1, part * 128 : (part + 1) * 128]
                filters[f, k, part] = jnp.broadcast_to(row, (ROWS, 128))

    to_right.wait()
    to_left.wait()
    for n in range(CHUNKS):
        offset = slab_of(s, v) * SLAB + n * ROWS
        for x in range(2):
            lefts = flag_column(near_flags[0, x : x + 1, :], offset)
            rights = flag_column(near_flags[1, x : x + 1, :], offset)
            marks[n, x] = jnp.broadcast_to(jnp.where(s == 0, 4.0, lefts), (ROWS, PLANE))
            marks[n, 2 + x] = jnp.broadcast_to(flag_column(flags[x : x + 1, :], offset), (ROWS, PLANE))
            marks[n, 4 + x] = jnp.broadcast_to(jnp.where(s == total - 1, 4.0, rights), (ROWS, PLANE))

    def exchange(phase, n, src, left_dst, right_dst):
        at = phase * CHUNKS + n
        one = remote(src.at[n, 4:8], left_dst.at[n], halo_send.at[at, 0], halo_recv.at[at, 0], right)
        two = remote(src.at[n, 0:4], right_dst.at[n], halo_send.at[at, 1], halo_recv.at[at, 1], left)
        one.start()
        two.start()
        return [one, two]

    def arrived(n):
        for u in range(PEERS):
            pltpu.make_async_copy(recv.at[n, u], recv.at[n, u], in_recv.at[n, u]).wait()

    def work(n):
        def put_moved(u, part, zero, one):
            at = pl.multiple_of((2 * u + part) * 2 * ROWS, 2 * ROWS)
            moved[pl.ds(at, ROWS), :] = zero
            moved[pl.ds(at + ROWS, ROWS), :] = one

        transport([marks[n, r] for r in range(6)], states, recv.at[n], left1.at[n], right1.at[n], put_moved)
        collide(filters, tab, moved, spec, modes, first, second, gain)
        for k in range(VG):
            for x in range(2):
                at = k * 2 * ROWS + x * ROWS
                lanes = slice((k % 2) * PLANE, (k % 2 + 1) * PLANE)
                coll[n, k // 2, x, :, lanes] = moved[at : at + ROWS, :] + 0.5 * gain[at : at + ROWS, :]

    def finish(n):
        def put_done(u, part, zero, one):
            lanes = slice(part * PLANE, (part + 1) * PLANE)
            done[n, u, 0, :, lanes] = zero
            done[n, u, 1, :, lanes] = one

        transport([marks[n, r] for r in range(6)], states, coll.at[n], left2.at[n], right2.at[n], put_done)
        for d, w in enumerate(peers):
            copy = remote(done.at[n, w], out.at[:, cells(v, n), :], out_send.at[n, d], out_recv.at[n, v], {"space": s, "vel": w})
            copy.start()
            sent.append(copy)
        pltpu.make_async_copy(done.at[n, v], out.at[:, cells(v, n), :], out_recv.at[n, v]).start()

    def settle(copies):
        for copy in copies:
            copy.wait()

    halos1, halos2 = {}, {}
    for n in range(CHUNKS):
        arrived(n)
        halos1[n] = exchange(0, n, recv, left1, right1)
        if n > 0:
            settle(halos2[n - 1])
            finish(n - 1)
        settle(halos1[n])
        work(n)
        halos2[n] = exchange(1, n, coll, left2, right2)
    settle(halos2[CHUNKS - 1])
    finish(CHUNKS - 1)
    for copy in sent:
        copy.wait_send()
    for n in range(CHUNKS):
        for u in range(PEERS):
            pltpu.make_async_copy(done.at[n, u], out.at[:, cells(u, n), :], out_recv.at[n, u]).wait()


def build(column, distribution, cell_flags, kernel_alpha, kernel_beta, kernel_loss, boundary_states):
    dims = (CHUNKS, PEERS, 2, ROWS, 2 * PLANE)
    side = (CHUNKS, PEERS // 2, 2, ROWS, 2 * PLANE)
    block = (VG * 2 * ROWS, PLANE)
    vmem = pl.BlockSpec(memory_space=pltpu.VMEM)
    anywhere = pl.BlockSpec(memory_space=pl.ANY)
    dma = pltpu.SemaphoreType.DMA
    states = boundary_states.reshape(2, PEERS, 2, PLANE).transpose(1, 0, 2, 3)
    return pl.pallas_call(
        functools.partial(step_kernel, column),
        out_shape=jax.ShapeDtypeStruct(distribution.shape, f32),
        in_specs=[anywhere] + [vmem] * 6,
        out_specs=anywhere,
        scratch_shapes=[
            pltpu.VMEM(dims, f32),
            pltpu.VMEM(side, f32),
            pltpu.VMEM(side, f32),
            pltpu.VMEM(dims, f32),
            pltpu.VMEM(side, f32),
            pltpu.VMEM(side, f32),
            pltpu.VMEM(dims, f32),
        ]
        + [pltpu.VMEM(block, f32)] * 6
        + [
            pltpu.VMEM((FILTERS * VG, PLANE), f32),
            pltpu.VMEM((FILTERS, VG, 2, ROWS, 128), f32),
            pltpu.VMEM((2, 2, 128), jnp.int32),
            pltpu.VMEM((CHUNKS, 6, ROWS, PLANE), f32),
            dma((CHUNKS, PEERS)),
            dma((CHUNKS, PEERS)),
            dma((CHUNKS, PEERS)),
            dma((CHUNKS, PEERS)),
            dma((2 * CHUNKS, 2)),
            dma((2 * CHUNKS, 2)),
            dma((2,)),
            dma((2,)),
        ],
        compiler_params=pltpu.CompilerParams(
            collective_id=0, has_side_effects=True, vmem_limit_bytes=48 * 1024 * 1024
        ),
    )(distribution, cell_flags, kernel_alpha, kernel_beta, kernel_loss.reshape(VG, PLANE), states, jnp.asarray(tables()))


def solution(mesh, column=COLUMN):
    return jax.shard_map(
        functools.partial(build, column),
        mesh=mesh,
        in_specs=(P("space", None, "vel"), P("space", None), P(), P(), P(), P()),
        out_specs=P("space", None, "vel"),
        check_vma=False,
    )
```

```python
import functools

import jax
import jax.numpy as jnp
import numpy as np
from jax import lax
from jax.experimental import pallas as pl
from jax.experimental.pallas import tpu as pltpu
from jax.sharding import PartitionSpec as P

VG = 16
PLANE = VG * VG
VEL = VG * PLANE
DIRS = 8
FILTERS = 2 * DIRS + 1
PEERS = 8
TURNS = 4
GROUP = TURNS * PEERS
ROWS = 8
CHUNKS = 2
MESH = pl.DeviceIdType.MESH
f32 = jnp.float32
bf16 = jnp.bfloat16


def half_modes():
    own = [((0, 0), (0, 8)), ((8, 0), (8, 8))]
    seen, pairs = set(), []
    for a in range(VG):
        for b in range(VG):
            twin = ((-a) % VG, (-b) % VG)
            if twin == (a, b) or twin in seen:
                continue
            seen.add((a, b))
            pairs.append((a, b))
    return own, pairs


def tables():
    own, pairs = half_modes()
    j, l = np.meshgrid(np.arange(VG), np.arange(VG), indexing="ij")
    j, l = j.reshape(-1), l.reshape(-1)

    def angle(mode):
        return ((mode[0] * j + mode[1] * l) % VG) * (2.0 * np.pi / VG)

    forward = np.zeros((PLANE, PLANE))
    inverse = np.zeros((PLANE, PLANE))
    pick = np.zeros((PLANE, PLANE))
    half = PLANE // 2
    for lane, (first, second) in enumerate(own):
        forward[:, lane] = np.cos(angle(first))
        forward[:, half + lane] = np.cos(angle(second))
        inverse[lane] = np.cos(angle(first))
        inverse[half + lane] = np.cos(angle(second))
        one, two = (first[0] * VG + first[1], second[0] * VG + second[1])
        pick[one, lane] = pick[two, lane] = 0.5
        pick[one, half + lane], pick[two, half + lane] = 0.5, -0.5
    for lane, mode in enumerate(pairs, start=len(own)):
        forward[:, lane] = np.cos(angle(mode))
        forward[:, half + lane] = -np.sin(angle(mode))
        inverse[lane] = 2.0 * np.cos(angle(mode))
        inverse[half + lane] = -2.0 * np.sin(angle(mode))
        pick[mode[0] * VG + mode[1], lane] = 1.0

    def parts(table):
        high = table.astype(np.float32).astype(bf16)
        low = (table - high.astype(np.float64)).astype(np.float32).astype(bf16)
        return [high, low]

    stack = parts(forward) + parts(inverse / VEL) + [pick.astype(bf16)]
    return np.stack(stack)


def times_root(re, im, power):
    power %= VG
    if power == 0:
        return re, im
    if power == 4:
        return im, -re
    c = float(np.cos(2.0 * np.pi * power / VG))
    s = float(np.sin(2.0 * np.pi * power / VG))
    if power == 2:
        return (re + im) * c, (im - re) * c
    if power == 6:
        return (im - re) * s, (re + im) * (-s)
    return re * c + im * s, im * c - re * s


def four_points(z):
    (ar, ai), (br, bi), (cr, ci), (dr, di) = z
    pr, pi_, mr, mi = ar + cr, ai + ci, ar - cr, ai - ci
    qr, qi, nr, ni = br + dr, bi + di, br - dr, bi - di
    return [(pr + qr, pi_ + qi), (mr + ni, mi - nr), (pr - qr, pi_ - qi), (mr - ni, mi + nr)]


def line_transform(z):
    mid = [four_points([z[4 * a + b] for a in range(4)]) for b in range(4)]
    out = [None] * VG
    for k in range(4):
        group = four_points([times_root(*mid[b][k], b * k) for b in range(4)])
        for m in range(4):
            out[k + 4 * m] = group[m]
    return out


def line_inverse(z):
    flipped = line_transform([(im, re) for re, im in z])
    return [(re, im) for im, re in flipped]


def split_two(x):
    high = x.astype(bf16)
    return high, (x - high.astype(f32)).astype(bf16)


def dot_three(x, high, low):
    x_high, x_low = split_two(x)
    dot = functools.partial(jnp.dot, preferred_element_type=f32)
    return dot(x_high, high) + (dot(x_low, high) + dot(x_high, low))


def row_ids(width):
    return lax.broadcasted_iota(jnp.int32, (ROWS, width), 0)


def roll(x, shift):
    return pltpu.roll(x, shift, 0)


def swap_halves(a, b):
    low = row_ids(a.shape[1]) < 4
    return jnp.where(low, a, roll(b, 4)), jnp.where(low, roll(a, 4), b)


def swap_pairs(a, b):
    low = row_ids(a.shape[1]) % 4 < 2
    return jnp.where(low, a, roll(b, 2)), jnp.where(low, roll(a, 6), b)


def turn_groups(tiles):
    a, b, c, d = tiles
    a, c = swap_halves(a, c)
    b, d = swap_halves(b, d)
    a, b = swap_pairs(a, b)
    c, d = swap_pairs(c, d)
    return [a, b, c, d]


def flag_tile(rows, offset):
    lanes = lax.broadcasted_iota(jnp.int32, (ROWS, 128), 1)
    ids = row_ids(128)
    wide = jnp.zeros((ROWS, 128), f32)
    for at, row in enumerate(rows):
        if row is not None:
            wide = jnp.where(ids // 2 == at, jnp.broadcast_to(row.astype(f32), (ROWS, 128)), wide)
    return jnp.sum(jnp.where(lanes == ids % 2 + offset, wide, 0.0), axis=1, keepdims=True)


def ghost(val, mark, low, high):
    return jnp.where(mark == 1.0, low, jnp.where(mark == 2.0, high, val))


def stencil(g, one, two, a, mark):
    second = (1.0 - 1.5 * a + 0.5 * a * a) * g + (2.0 * a - a * a) * one + (0.5 * a * a - 0.5 * a) * two
    return jnp.where(mark == 0.0, second, jnp.where(mark == 3.0, g - a * (g - one), g))


def transport(marks, states, tiles_of, halo_of, put, outer, inner):
    edge, mid = marks(1), marks(2)
    ids = row_ids(PLANE)

    def side(v, positive):
        tiles = tiles_of(v)
        outs = []
        for part in range(2):
            at = pl.ds(pl.multiple_of((2 * v + part) * PLANE, PLANE), PLANE)
            low, high = states[0:1, at], states[1:2, at]
            a = jnp.abs((2 * (2 * v + part) - 15).astype(f32)) * (0.9 / 15.0)
            e = ghost(tiles[part][0], edge, low, high)
            m = ghost(tiles[part][1], mid, low, high)
            new_e, new_m = None, None
            if inner:
                if positive:
                    one = jnp.where(ids < 2, roll(e, 6), roll(m, 2))
                    two = jnp.where(ids < 4, e, roll(m, 4))
                else:
                    one = jnp.where(ids < 6, roll(m, 6), roll(e, 2))
                    two = jnp.where(ids < 4, roll(m, 4), e)
                new_m = stencil(m, one, two, a, mid)
            if outer:
                if halo_of is None:
                    two = m
                else:
                    halo = halo_of(v, positive)
                    if positive == (part == 1):
                        halo = roll(halo, 4)
                    mark = marks(0) if positive else marks(3)
                    halo = ghost(jnp.where(mark == 4.0, 0.0, halo), mark, low, high)
                    two = jnp.where((ids < 4) == positive, halo, m)
                if positive:
                    one = jnp.where(ids % 4 < 2, roll(two, 6), roll(e, 2))
                else:
                    one = jnp.where(ids % 4 < 2, roll(e, 6), roll(two, 2))
                new_e = stencil(e, one, two, a, edge)
            outs.append((new_e, new_m))
        put(v, positive, outs)

    @pl.loop(0, 4)
    def _(v):
        side(v, False)

    @pl.loop(4, 8)
    def _(v):
        side(v, True)


def collide(filters, tab, moved, spec, modes, first, second, gain):
    half = PLANE // 2
    rows = VG * ROWS

    def piece(ref, k, base=0):
        at = base + k * ROWS
        return ref[at : at + ROWS, 0:half], ref[at : at + ROWS, half:PLANE]

    def put(ref, k, val, base=0):
        at = base + k * ROWS
        ref[at : at + ROWS, 0:half] = val[0]
        ref[at : at + ROWS, half:PLANE] = val[1]

    spec[...] = dot_three(moved[...], tab[0], tab[1])
    done = line_transform([piece(spec, k) for k in range(VG)])
    for k in range(VG):
        put(modes, k, done[k])

    def filtered(index, target, base):
        z = [piece(modes, k) for k in range(VG)]
        w = []
        for k in range(VG):
            near, far = filters[index, k, 0], filters[index, k, 1]
            twin = z[-k % VG]
            w.append((near * z[k][0] + far * twin[0], near * z[k][1] - far * twin[1]))
        done = line_inverse(w)
        for k in range(VG):
            put(target, k, done[k], base)

    def both(p, target):
        filtered(p, target, 0)
        filtered(p + DIRS, target, rows)

    def product(source):
        got = dot_three(source[...], tab[2], tab[3])
        return got[0:rows] * got[rows:]

    filtered(2 * DIRS, second, 0)
    both(0, first)
    loss = dot_three(second[0:rows, :], tab[2], tab[3])
    gain[...] = -(moved[...] * loss)

    @pl.loop(0, DIRS // 2 - 1)
    def _(h):
        both(2 * h + 1, second)
        gain[...] += product(first)
        both(2 * h + 2, first)
        gain[...] += product(second)

    both(DIRS - 1, second)
    gain[...] += product(first)
    gain[...] += product(second)


def step_kernel(
    dist_in, flags_in, alpha_in, beta_in, loss_in, states_in, tab_in, out,
    dist, flags, alpha, beta, loss, states, tab, load_sem,
    pack_in, recv, left1, right1, coll, edge_out, left2, right2, pack_out, back, result,
    moved, spec, modes, first, second, gain, packed, filters, near, edge, marks,
    in_send, in_recv, out_send, out_recv, halo_send, halo_recv, flag_send, flag_recv, own_sem,
):
    s, v = lax.axis_index("space"), lax.axis_index("vel")
    total = lax.axis_size("space")
    group, turn = s // TURNS, s % TURNS
    upper = group % 2
    me = turn * PEERS + v

    def mirror(peer):
        return (3 - peer // 2) * 2 + peer % 2

    def block_of(t, peer):
        return (peer + upper * (mirror(peer) - peer)) * TURNS + t

    def peer_at(q):
        return {"space": group * TURNS + q // PEERS, "vel": q % PEERS}

    right = {"space": (s + TURNS) % total, "vel": mirror(v)}
    left = {"space": (s + total - TURNS) % total, "vel": mirror(v)}
    mine = block_of(turn, v)

    loads = [
        pltpu.make_async_copy(src, dst, load_sem.at[i])
        for i, (src, dst) in enumerate(
            [(dist_in, dist), (flags_in, flags), (alpha_in, alpha), (beta_in, beta), (loss_in, loss), (states_in, states), (tab_in, tab)]
        )
    ]
    for copy in loads:
        copy.start()
    barrier = pltpu.get_barrier_semaphore()

    @pl.loop(1, GROUP)
    def _(d):
        pl.semaphore_signal(barrier, inc=1, device_id=peer_at((me + d) % GROUP), device_id_type=MESH)

    for at in (left, right):
        pl.semaphore_signal(barrier, inc=1, device_id=at, device_id_type=MESH)

    loads[0].wait()

    @pl.loop(0, GROUP // 2)
    def _(b):
        at = pl.ds(pl.multiple_of(b * ROWS, ROWS), ROWS)
        turned = turn_groups([dist[x, at, part * PLANE : (part + 1) * PLANE] for part in range(2) for x in range(2)])
        for j in range(4):
            pack_in[j % 2, 2 * b + j // 2] = turned[j]

    for copy in loads[1:]:
        copy.wait()
    pl.semaphore_wait(barrier, GROUP + 1)

    def remote(src, dst, send, rec, at):
        return pltpu.make_async_remote_copy(
            src_ref=src, dst_ref=dst, send_sem=send, recv_sem=rec, device_id=at, device_id_type=MESH
        )

    for d in range(1, TURNS):
        at = {"space": group * TURNS + (turn + d) % TURNS, "vel": v}
        remote(flags, near.at[turn], flag_send.at[0], flag_recv.at[0], at).start()
    pltpu.make_async_copy(flags, near.at[turn], flag_recv.at[0]).start()

    for n in range(CHUNKS):

        @pl.loop(1, GROUP)
        def _(d):
            q = (me + d) % GROUP
            src = pack_in.at[n, block_of(q // PEERS, q % PEERS)]
            remote(src, recv.at[n, turn, v], in_send.at[n], in_recv.at[n], peer_at(q)).start()

        pltpu.make_async_copy(pack_in.at[n, mine], recv.at[n, turn, v], in_recv.at[n]).start()

    def pick(rest):
        got = jnp.zeros(rest.shape, f32)
        for _ in range(3):
            one = rest.astype(bf16)
            rest = rest - one.astype(f32)
            got = got + jnp.dot(one, tab[4], preferred_element_type=f32)
        return got

    def by_line(ref):
        return jnp.concatenate([ref[:, k * PLANE : (k + 1) * PLANE] for k in range(VG)], 0)

    packed[0 : VG * DIRS, :] = pick(by_line(alpha))
    packed[VG * DIRS : 2 * VG * DIRS, :] = pick(by_line(beta))
    packed[2 * VG * DIRS :, :] = pick(by_line(loss))
    for k in range(VG):
        for f in range(FILTERS):
            at = 2 * VG * DIRS + k if f == 2 * DIRS else (f // DIRS) * VG * DIRS + k * DIRS + f % DIRS
            for part in range(2):
                row = packed[at : at + 1, part * 128 : (part + 1) * 128]
                filters[f, k, part] = jnp.broadcast_to(row, (ROWS, 128))

    pltpu.make_async_copy(near, near, flag_recv.at[0]).wait()
    edges = [
        remote(near.at[3], edge.at[0], flag_send.at[1], flag_recv.at[1], right),
        remote(near.at[0], edge.at[1], flag_send.at[2], flag_recv.at[2], left),
    ]
    for copy in edges:
        copy.start()
    offset = mine * 4
    for n in range(CHUNKS):
        for at, pair in ((1, (0, 3)), (2, (1, 2))):
            rows = [near[pair[r // 2], r % 2 : r % 2 + 1, :] for r in range(4)]
            marks[n, at] = jnp.broadcast_to(flag_tile(rows, offset + 2 * n), (ROWS, PLANE))

    def exchange(at, ups, downs, ups_dst, downs_dst):
        one = remote(ups, ups_dst, halo_send.at[at, 0], halo_recv.at[at, 0], right)
        two = remote(downs, downs_dst, halo_send.at[at, 1], halo_recv.at[at, 1], left)
        one.start()
        two.start()
        return [one, two]

    def settle(copies):
        for copy in copies:
            copy.wait()

    def begin(n):
        pltpu.make_async_copy(recv.at[n], recv.at[n], in_recv.at[n]).wait()
        return exchange(n, recv.at[n, 3, 4:8], recv.at[n, 0, 0:4], left1.at[n], right1.at[n])

    def work(n, which):
        def tiles_of(u):
            one = swap_halves(recv[n, 0, u], recv[n, 3, u])
            two = swap_halves(recv[n, 1, u], recv[n, 2, u])
            return [(one[part], two[part]) for part in range(2)]

        def halo_of(u, positive):
            return left1[n, u - 4] if positive else right1[n, u]

        def put_moved(u, positive, outs):
            for part in range(2):
                at = pl.multiple_of((2 * u + part) * ROWS, ROWS)
                moved[pl.ds(at, ROWS), :] = outs[part][which]

        transport(lambda r: marks[n, r], states, tiles_of, halo_of, put_moved, which == 0, which == 1)
        collide(filters, tab, moved, spec, modes, first, second, gain)
        for u in range(PEERS):
            pair = []
            for part in range(2):
                at = (2 * u + part) * ROWS
                pair.append(moved[at : at + ROWS, :] + 0.5 * gain[at : at + ROWS, :])
                coll[n, u, part, which] = pair[part]
            if which == 0 and u < 4:
                edge_out[n, 1, u] = swap_halves(*pair)[0]
            if which == 0 and u >= 4:
                edge_out[n, 0, u - 4] = swap_halves(*pair)[1]

    def pass_on(n):
        return exchange(CHUNKS + n, edge_out.at[n, 0], edge_out.at[n, 1], left2.at[n], right2.at[n])

    def give(n, t, u):
        q = t * PEERS + u

        @pl.when(q != me)
        def _():
            remote(pack_out.at[n, t, u], back.at[n, mine], out_send.at[n], out_recv.at[n], peer_at(q)).start()

        @pl.when(q == me)
        def _():
            pltpu.make_async_copy(pack_out.at[n, t, u], back.at[n, mine], out_recv.at[n]).start()

    def collided(n):
        def tiles_of(u):
            return [(coll[n, u, part, 0], coll[n, u, part, 1]) for part in range(2)]

        return tiles_of

    def finish_most(n):
        def put_done(u, positive, outs):
            one, two = swap_halves(outs[0][1], outs[1][1])
            pack_out[n, 1, u] = one
            pack_out[n, 2, u] = two
            ends = swap_halves(outs[0][0], outs[1][0])
            if positive:
                pack_out[n, 3, u] = ends[1]
            else:
                pack_out[n, 0, u] = ends[0]

        transport(lambda r: marks[n, r], states, collided(n), None, put_done, True, True)

        @pl.loop(0, 3 * PEERS)
        def _(d):
            u = (v + 1 + d) % PEERS
            give(n, (turn + d // PEERS) % 3 + u // 4, u)

    def finish_rest(n):
        def halo_of(u, positive):
            return left2[n, u - 4] if positive else right2[n, u]

        def put_done(u, positive, outs):
            ends = swap_halves(outs[0][0], outs[1][0])
            if positive:
                pack_out[n, 0, u] = ends[0]
            else:
                pack_out[n, 3, u] = ends[1]

        transport(lambda r: marks[n, r], states, collided(n), halo_of, put_done, True, False)

        @pl.loop(0, PEERS)
        def _(d):
            u = (v + 1 + d) % PEERS
            give(n, 3 - 3 * (u // 4), u)

    one1 = begin(0)
    work(0, 1)
    settle(edges)
    for n in range(CHUNKS):
        lefts = flag_tile([edge[0, 0:1, :], edge[0, 1:2, :], None, None], offset + 2 * n)
        rights = flag_tile([None, None, edge[1, 0:1, :], edge[1, 1:2, :]], offset + 2 * n)
        marks[n, 0] = jnp.broadcast_to(jnp.where(group == 0, 4.0, lefts), (ROWS, PLANE))
        marks[n, 3] = jnp.broadcast_to(jnp.where(group == total // TURNS - 1, 4.0, rights), (ROWS, PLANE))
    settle(one1)
    work(0, 0)
    one2 = pass_on(0)
    two1 = begin(1)
    finish_most(0)
    work(1, 1)
    settle(one2)
    finish_rest(0)
    settle(two1)
    work(1, 0)
    two2 = pass_on(1)
    finish_most(1)
    settle(two2)
    finish_rest(1)
    for n in range(CHUNKS):
        pltpu.make_async_copy(back.at[n], back.at[n], out_recv.at[n]).wait()

    @pl.loop(0, GROUP // 2)
    def _(b):
        at = pl.ds(pl.multiple_of(b * ROWS, ROWS), ROWS)
        turned = turn_groups([back[j % 2, 2 * b + j // 2] for j in range(4)])
        for part in range(2):
            for x in range(2):
                result[x, at, part * PLANE : (part + 1) * PLANE] = turned[2 * part + x]

    last = pltpu.make_async_copy(result, out, own_sem)
    last.start()
    for n in range(CHUNKS):
        for buf, sem in ((pack_in, in_send), (back, out_send)):
            pltpu.make_async_copy(buf.at[n, 0 : GROUP - 1], buf.at[n, 0 : GROUP - 1], sem.at[n]).wait()
    pltpu.make_async_copy(near.at[0:3], near.at[0:3], flag_send.at[0]).wait()
    last.wait()


def build(distribution, cell_flags, kernel_alpha, kernel_beta, kernel_loss, boundary_states):
    tile = (ROWS, PLANE)
    block = (VG * ROWS, PLANE)
    double = (2 * VG * ROWS, PLANE)
    anywhere = pl.BlockSpec(memory_space=pl.ANY)
    dma = pltpu.SemaphoreType.DMA

    def room(*dims):
        return pltpu.VMEM(dims + tile, f32)

    return pl.pallas_call(
        step_kernel,
        out_shape=jax.ShapeDtypeStruct(distribution.shape, f32),
        in_specs=[anywhere] * 7,
        out_specs=anywhere,
        scratch_shapes=[
            pltpu.VMEM(distribution.shape, f32),
            pltpu.VMEM((2, 128), jnp.int32),
            pltpu.VMEM((DIRS, VEL), f32),
            pltpu.VMEM((DIRS, VEL), f32),
            pltpu.VMEM((1, VEL), f32),
            pltpu.VMEM((2, VEL), f32),
            pltpu.VMEM((5, PLANE, PLANE), bf16),
            dma((7,)),
            room(CHUNKS, GROUP),
            room(CHUNKS, TURNS, PEERS),
            room(CHUNKS, PEERS // 2),
            room(CHUNKS, PEERS // 2),
            room(CHUNKS, PEERS, 2, 2),
            room(CHUNKS, 2, PEERS // 2),
            room(CHUNKS, PEERS // 2),
            room(CHUNKS, PEERS // 2),
            room(CHUNKS, TURNS, PEERS),
            room(CHUNKS, GROUP),
            pltpu.VMEM(distribution.shape, f32),
        ]
        + [pltpu.VMEM(block, f32)] * 3
        + [pltpu.VMEM(double, f32)] * 2
        + [pltpu.VMEM(block, f32)]
        + [
            pltpu.VMEM((FILTERS * VG, PLANE), f32),
            pltpu.VMEM((FILTERS, VG, 2, ROWS, 128), f32),
            pltpu.VMEM((TURNS, 2, 128), jnp.int32),
            pltpu.VMEM((2, 2, 128), jnp.int32),
            room(CHUNKS, 4),
            dma((CHUNKS,)),
            dma((CHUNKS,)),
            dma((CHUNKS,)),
            dma((CHUNKS,)),
            dma((2 * CHUNKS, 2)),
            dma((2 * CHUNKS, 2)),
            dma((3,)),
            dma((3,)),
            dma(()),
        ],
        compiler_params=pltpu.CompilerParams(collective_id=0, has_side_effects=True),
    )(distribution, cell_flags, kernel_alpha, kernel_beta, kernel_loss.reshape(1, VEL), boundary_states, jnp.asarray(tables()))


def solution(mesh):
    return jax.shard_map(
        build,
        mesh=mesh,
        in_specs=(P("space", None, "vel"), P("space", None), P(), P(), P(), P()),
        out_specs=P("space", None, "vel"),
        check_vma=False,
    )
```

```python
import functools

import jax
import jax.numpy as jnp
import numpy as np
from jax import lax
from jax.experimental import pallas as pl
from jax.experimental.pallas import tpu as pltpu
from jax.sharding import PartitionSpec as P

VG = 16
PLANE = VG * VG
VEL = VG * PLANE
DIRS = 8
FILTERS = 2 * DIRS + 1
PEERS = 8
TURNS = 4
GROUP = TURNS * PEERS
ROWS = 8
CHUNKS = 2
MESH = pl.DeviceIdType.MESH
f32 = jnp.float32
bf16 = jnp.bfloat16


def half_modes():
    own = [((0, 0), (0, 8)), ((8, 0), (8, 8))]
    seen, pairs = set(), []
    for a in range(VG):
        for b in range(VG):
            twin = ((-a) % VG, (-b) % VG)
            if twin == (a, b) or twin in seen:
                continue
            seen.add((a, b))
            pairs.append((a, b))
    return own, pairs


def tables():
    own, pairs = half_modes()
    j, l = np.meshgrid(np.arange(VG), np.arange(VG), indexing="ij")
    j, l = j.reshape(-1), l.reshape(-1)

    def angle(mode):
        return ((mode[0] * j + mode[1] * l) % VG) * (2.0 * np.pi / VG)

    forward = np.zeros((PLANE, PLANE))
    inverse = np.zeros((PLANE, PLANE))
    pick = np.zeros((PLANE, PLANE))
    half = PLANE // 2
    for lane, (first, second) in enumerate(own):
        forward[:, lane] = np.cos(angle(first))
        forward[:, half + lane] = np.cos(angle(second))
        inverse[lane] = np.cos(angle(first))
        inverse[half + lane] = np.cos(angle(second))
        one, two = (first[0] * VG + first[1], second[0] * VG + second[1])
        pick[one, lane] = pick[two, lane] = 0.5
        pick[one, half + lane], pick[two, half + lane] = 0.5, -0.5
    for lane, mode in enumerate(pairs, start=len(own)):
        forward[:, lane] = np.cos(angle(mode))
        forward[:, half + lane] = -np.sin(angle(mode))
        inverse[lane] = 2.0 * np.cos(angle(mode))
        inverse[half + lane] = -2.0 * np.sin(angle(mode))
        pick[mode[0] * VG + mode[1], lane] = 1.0

    def parts(table):
        high = table.astype(np.float32).astype(bf16)
        low = (table - high.astype(np.float64)).astype(np.float32).astype(bf16)
        return [high, low]

    stack = parts(forward) + parts(inverse / VEL) + [pick.astype(bf16)]
    return np.stack(stack)


def times_root(re, im, power):
    power %= VG
    if power == 0:
        return re, im
    if power == 4:
        return im, -re
    c = float(np.cos(2.0 * np.pi * power / VG))
    s = float(np.sin(2.0 * np.pi * power / VG))
    if power == 2:
        return (re + im) * c, (im - re) * c
    if power == 6:
        return (im - re) * s, (re + im) * (-s)
    return re * c + im * s, im * c - re * s


def four_points(z):
    (ar, ai), (br, bi), (cr, ci), (dr, di) = z
    pr, pi_, mr, mi = ar + cr, ai + ci, ar - cr, ai - ci
    qr, qi, nr, ni = br + dr, bi + di, br - dr, bi - di
    return [(pr + qr, pi_ + qi), (mr + ni, mi - nr), (pr - qr, pi_ - qi), (mr - ni, mi + nr)]


def line_transform(z):
    mid = [four_points([z[4 * a + b] for a in range(4)]) for b in range(4)]
    out = [None] * VG
    for k in range(4):
        group = four_points([times_root(*mid[b][k], b * k) for b in range(4)])
        for m in range(4):
            out[k + 4 * m] = group[m]
    return out


def line_inverse(z):
    flipped = line_transform([(im, re) for re, im in z])
    return [(re, im) for im, re in flipped]


def split_two(x):
    high = x.astype(bf16)
    return high, (x - high.astype(f32)).astype(bf16)


def dot_three(x, high, low):
    x_high, x_low = split_two(x)
    dot = functools.partial(jnp.dot, preferred_element_type=f32)
    return dot(x_high, high) + (dot(x_low, high) + dot(x_high, low))


def row_ids(width):
    return lax.broadcasted_iota(jnp.int32, (ROWS, width), 0)


def roll(x, shift):
    return pltpu.roll(x, shift, 0)


def swap_halves(a, b):
    low = row_ids(a.shape[1]) < 4
    return jnp.where(low, a, roll(b, 4)), jnp.where(low, roll(a, 4), b)


def swap_pairs(a, b):
    low = row_ids(a.shape[1]) % 4 < 2
    return jnp.where(low, a, roll(b, 2)), jnp.where(low, roll(a, 6), b)


def turn_groups(tiles):
    a, b, c, d = tiles
    a, c = swap_halves(a, c)
    b, d = swap_halves(b, d)
    a, b = swap_pairs(a, b)
    c, d = swap_pairs(c, d)
    return [a, b, c, d]


def flag_tile(rows, offset):
    lanes = lax.broadcasted_iota(jnp.int32, (ROWS, 128), 1)
    ids = row_ids(128)
    wide = jnp.zeros((ROWS, 128), f32)
    for at, row in enumerate(rows):
        if row is not None:
            wide = jnp.where(ids // 2 == at, jnp.broadcast_to(row.astype(f32), (ROWS, 128)), wide)
    return jnp.sum(jnp.where(lanes == ids % 2 + offset, wide, 0.0), axis=1, keepdims=True)


def ghost(val, mark, low, high):
    return jnp.where(mark == 1.0, low, jnp.where(mark == 2.0, high, val))


def stencil(g, one, two, a, mark):
    second = (1.0 - 1.5 * a + 0.5 * a * a) * g + (2.0 * a - a * a) * one + (0.5 * a * a - 0.5 * a) * two
    return jnp.where(mark == 0.0, second, jnp.where(mark == 3.0, g - a * (g - one), g))


def transport(marks, states, tiles_of, halo_of, put, outer, inner):
    edge, mid = marks(1), marks(2)
    ids = row_ids(PLANE)

    def side(v, positive):
        tiles = tiles_of(v)
        outs = []
        for part in range(2):
            at = pl.ds(pl.multiple_of((2 * v + part) * PLANE, PLANE), PLANE)
            low, high = states[0:1, at], states[1:2, at]
            a = jnp.abs((2 * (2 * v + part) - 15).astype(f32)) * (0.9 / 15.0)
            e = ghost(tiles[part][0], edge, low, high)
            m = ghost(tiles[part][1], mid, low, high)
            new_e, new_m = None, None
            if inner:
                if positive:
                    one = jnp.where(ids < 2, roll(e, 6), roll(m, 2))
                    two = jnp.where(ids < 4, e, roll(m, 4))
                else:
                    one = jnp.where(ids < 6, roll(m, 6), roll(e, 2))
                    two = jnp.where(ids < 4, roll(m, 4), e)
                new_m = stencil(m, one, two, a, mid)
            if outer:
                if halo_of is None:
                    two = m
                else:
                    halo = halo_of(v, positive)
                    if positive == (part == 1):
                        halo = roll(halo, 4)
                    mark = marks(0) if positive else marks(3)
                    halo = ghost(jnp.where(mark == 4.0, 0.0, halo), mark, low, high)
                    two = jnp.where((ids < 4) == positive, halo, m)
                if positive:
                    one = jnp.where(ids % 4 < 2, roll(two, 6), roll(e, 2))
                else:
                    one = jnp.where(ids % 4 < 2, roll(e, 6), roll(two, 2))
                new_e = stencil(e, one, two, a, edge)
            outs.append((new_e, new_m, e))
        put(v, positive, outs)

    @pl.loop(0, 4)
    def _(v):
        side(v, False)

    @pl.loop(4, 8)
    def _(v):
        side(v, True)


def collide(filters, tab, moved, spec, modes, first, second, gain):
    half = PLANE // 2
    rows = VG * ROWS

    def piece(ref, k, base=0):
        at = base + k * ROWS
        return ref[at : at + ROWS, 0:half], ref[at : at + ROWS, half:PLANE]

    def put(ref, k, val, base=0):
        at = base + k * ROWS
        ref[at : at + ROWS, 0:half] = val[0]
        ref[at : at + ROWS, half:PLANE] = val[1]

    spec[...] = dot_three(moved[...], tab[0], tab[1])
    done = line_transform([piece(spec, k) for k in range(VG)])
    for k in range(VG):
        put(modes, k, done[k])

    def filtered(index, target, base):
        z = [piece(modes, k) for k in range(VG)]
        w = []
        for k in range(VG):
            near, far = filters[index, k, 0], filters[index, k, 1]
            twin = z[-k % VG]
            w.append((near * z[k][0] + far * twin[0], near * z[k][1] - far * twin[1]))
        done = line_inverse(w)
        for k in range(VG):
            put(target, k, done[k], base)

    def both(p, target):
        filtered(p, target, 0)
        filtered(p + DIRS, target, rows)

    def product(source):
        got = dot_three(source[...], tab[2], tab[3])
        return got[0:rows] * got[rows:]

    filtered(2 * DIRS, second, 0)
    both(0, first)
    loss = dot_three(second[0:rows, :], tab[2], tab[3])
    gain[...] = -(moved[...] * loss)

    @pl.loop(0, DIRS // 2 - 1)
    def _(h):
        both(2 * h + 1, second)
        gain[...] += product(first)
        both(2 * h + 2, first)
        gain[...] += product(second)

    both(DIRS - 1, second)
    gain[...] += product(first)
    gain[...] += product(second)


def step_kernel(
    dist_in, flags_in, alpha_in, beta_in, loss_in, states_in, tab_in, out,
    dist, flags, alpha, beta, loss, states, tab, load_sem,
    pack_in, recv, left1, right1, coll, pack_far, far, pack_out, back, result,
    moved, spec, modes, first, second, gain, packed, filters, near, edge, marks, own_marks,
    in_send, in_recv, out_send, out_recv, far_send, far_recv, halo_send, halo_recv, flag_send, flag_recv, own_sem,
):
    s, v = lax.axis_index("space"), lax.axis_index("vel")
    total = lax.axis_size("space")
    group, turn = s // TURNS, s % TURNS
    upper = group % 2
    me = turn * PEERS + v

    def mirror(peer):
        return (peer + PEERS // 2) % PEERS

    def block_of(t, peer):
        return (peer + upper * (mirror(peer) - peer)) * TURNS + t

    def peer_at(q):
        return {"space": group * TURNS + q // PEERS, "vel": q % PEERS}

    right = {"space": (s + TURNS) % total, "vel": mirror(v)}
    left = {"space": (s + total - TURNS) % total, "vel": mirror(v)}
    mine = block_of(turn, v)

    loads = [
        pltpu.make_async_copy(src, dst, load_sem.at[i])
        for i, (src, dst) in enumerate(
            [(dist_in, dist), (flags_in, flags), (alpha_in, alpha), (beta_in, beta), (loss_in, loss), (states_in, states), (tab_in, tab)]
        )
    ]
    for copy in loads:
        copy.start()
    barrier = pltpu.get_barrier_semaphore()

    @pl.loop(1, GROUP)
    def _(d):
        pl.semaphore_signal(barrier, inc=1, device_id=peer_at((me + d) % GROUP), device_id_type=MESH)

    for at in (left, right):
        pl.semaphore_signal(barrier, inc=1, device_id=at, device_id_type=MESH)

    loads[0].wait()

    @pl.loop(0, GROUP // 2)
    def _(b):
        at = pl.ds(pl.multiple_of(b * ROWS, ROWS), ROWS)
        turned = turn_groups([dist[x, at, part * PLANE : (part + 1) * PLANE] for part in range(2) for x in range(2)])
        for j in range(4):
            pack_in[j % 2, 2 * b + j // 2] = turned[j]

    for copy in loads[1:]:
        copy.wait()
    pl.semaphore_wait(barrier, GROUP + 1)

    def remote(src, dst, send, rec, at):
        return pltpu.make_async_remote_copy(
            src_ref=src, dst_ref=dst, send_sem=send, recv_sem=rec, device_id=at, device_id_type=MESH
        )

    for d in range(1, TURNS):
        at = {"space": group * TURNS + (turn + d) % TURNS, "vel": v}
        remote(flags, near.at[turn], flag_send.at[0], flag_recv.at[0], at).start()
    pltpu.make_async_copy(flags, near.at[turn], flag_recv.at[0]).start()

    for n in range(CHUNKS):

        @pl.loop(1, GROUP)
        def _(d):
            q = (me + d) % GROUP
            src = pack_in.at[n, block_of(q // PEERS, q % PEERS)]
            remote(src, recv.at[n, turn, v], in_send.at[n], in_recv.at[n], peer_at(q)).start()

        pltpu.make_async_copy(pack_in.at[n, mine], recv.at[n, turn, v], in_recv.at[n]).start()

    def pick(rest):
        got = jnp.zeros(rest.shape, f32)
        for _ in range(3):
            one = rest.astype(bf16)
            rest = rest - one.astype(f32)
            got = got + jnp.dot(one, tab[4], preferred_element_type=f32)
        return got

    def by_line(ref):
        return jnp.concatenate([ref[:, k * PLANE : (k + 1) * PLANE] for k in range(VG)], 0)

    packed[0 : VG * DIRS, :] = pick(by_line(alpha))
    packed[VG * DIRS : 2 * VG * DIRS, :] = pick(by_line(beta))
    packed[2 * VG * DIRS :, :] = pick(by_line(loss))
    for k in range(VG):
        for f in range(FILTERS):
            at = 2 * VG * DIRS + k if f == 2 * DIRS else (f // DIRS) * VG * DIRS + k * DIRS + f % DIRS
            for part in range(2):
                row = packed[at : at + 1, part * 128 : (part + 1) * 128]
                filters[f, k, part] = jnp.broadcast_to(row, (ROWS, 128))

    pltpu.make_async_copy(near, near, flag_recv.at[0]).wait()
    edges = [
        remote(near.at[3], edge.at[0], flag_send.at[1], flag_recv.at[1], right),
        remote(near.at[0], edge.at[1], flag_send.at[2], flag_recv.at[2], left),
    ]
    for copy in edges:
        copy.start()
    offset = mine * 4
    for n in range(CHUNKS):
        for at, pair in ((1, (0, 3)), (2, (1, 2))):
            rows = [near[pair[r // 2], r % 2 : r % 2 + 1, :] for r in range(4)]
            marks[n, at] = jnp.broadcast_to(flag_tile(rows, offset + 2 * n), (ROWS, PLANE))

    for x in range(2):
        wide = jnp.broadcast_to(flags[x : x + 1, :].astype(f32), (ROWS, 128))
        lanes = lax.broadcasted_iota(jnp.int32, (ROWS, 128), 1)
        for b in range(GROUP // 2):
            column = jnp.sum(jnp.where(lanes == row_ids(128) + b * ROWS, wide, 0.0), axis=1, keepdims=True)
            own_marks[x, b * ROWS : (b + 1) * ROWS, :] = jnp.broadcast_to(column, (ROWS, 128))

    def exchange(at, ups, downs, ups_dst, downs_dst):
        one = remote(ups, ups_dst, halo_send.at[at, 0], halo_recv.at[at, 0], right)
        two = remote(downs, downs_dst, halo_send.at[at, 1], halo_recv.at[at, 1], left)
        one.start()
        two.start()
        return [one, two]

    def settle(copies):
        for copy in copies:
            copy.wait()

    def begin(n):
        pltpu.make_async_copy(recv.at[n], recv.at[n], in_recv.at[n]).wait()
        return exchange(n, recv.at[n, 3, 4:8], recv.at[n, 0, 0:4], left1.at[n], right1.at[n])

    def work(n, which):
        def tiles_of(u):
            one = swap_halves(recv[n, 0, u], recv[n, 3, u])
            two = swap_halves(recv[n, 1, u], recv[n, 2, u])
            return [(one[part], two[part]) for part in range(2)]

        def halo_of(u, positive):
            return left1[n, u - 4] if positive else right1[n, u]

        def put_moved(u, positive, outs):
            for part in range(2):
                at = pl.multiple_of((2 * u + part) * ROWS, ROWS)
                moved[pl.ds(at, ROWS), :] = outs[part][which]

        transport(lambda r: marks[n, r], states, tiles_of, halo_of, put_moved, which == 0, which == 1)
        collide(filters, tab, moved, spec, modes, first, second, gain)
        for u in range(PEERS):
            pair = []
            for part in range(2):
                at = (2 * u + part) * ROWS
                pair.append(moved[at : at + ROWS, :] + 0.5 * gain[at : at + ROWS, :])
                coll[n, u, part, which] = pair[part]

    def collided(n):
        def tiles_of(u):
            return [(coll[n, u, part, 0], coll[n, u, part, 1]) for part in range(2)]

        return tiles_of

    def finish(n):
        def put_done(u, positive, outs):
            one, two = swap_halves(outs[0][1], outs[1][1])
            pack_out[n, 1, u] = one
            pack_out[n, 2, u] = two
            ends = swap_halves(outs[0][0], outs[1][0])
            raw = swap_halves(outs[0][2], outs[1][2])
            if positive:
                pack_out[n, 3, u] = ends[1]
                pack_out[n, 0, u] = raw[0]
                pack_far[n, u] = raw[1]
            else:
                pack_out[n, 0, u] = ends[0]
                pack_out[n, 3, u] = raw[1]
                pack_far[n, u] = raw[0]

        transport(lambda r: marks[n, r], states, collided(n), None, put_done, True, True)

        @pl.loop(0, PEERS)
        def _(d):
            u = (v + d) % PEERS
            at = (s - turn + total + TURNS * (2 * (u // 4) - 1)) % total + 3 * (1 - u // 4)
            remote(pack_far.at[n, u], far.at[n, mine], far_send.at[n], far_recv.at[n], {"space": at, "vel": u}).start()

        @pl.loop(1, GROUP)
        def _(d):
            q = (me + d) % GROUP
            src = pack_out.at[n, q // PEERS, q % PEERS]
            remote(src, back.at[n, mine], out_send.at[n], out_recv.at[n], peer_at(q)).start()

        pltpu.make_async_copy(pack_out.at[n, turn, v], back.at[n, mine], out_recv.at[n]).start()

    one1 = begin(0)
    work(0, 1)
    settle(edges)
    for n in range(CHUNKS):
        lefts = flag_tile([edge[0, 0:1, :], edge[0, 1:2, :], None, None], offset + 2 * n)
        rights = flag_tile([None, None, edge[1, 0:1, :], edge[1, 1:2, :]], offset + 2 * n)
        marks[n, 0] = jnp.broadcast_to(jnp.where(group == 0, 4.0, lefts), (ROWS, PLANE))
        marks[n, 3] = jnp.broadcast_to(jnp.where(group == total // TURNS - 1, 4.0, rights), (ROWS, PLANE))
    settle(one1)
    work(0, 0)
    two1 = begin(1)
    finish(0)
    work(1, 1)
    settle(two1)
    work(1, 0)
    finish(1)
    for n in range(CHUNKS):
        pltpu.make_async_copy(back.at[n], back.at[n], out_recv.at[n]).wait()
    up_end = jnp.logical_and(turn == 0, v >= PEERS // 2)
    down_end = jnp.logical_and(turn == TURNS - 1, v < PEERS // 2)

    def unpack(b, fix):
        at = pl.ds(pl.multiple_of(b * ROWS, ROWS), ROWS)
        turned = turn_groups([back[j % 2, 2 * b + j // 2] for j in range(4)])
        if fix is not None:
            turned = fix(at, turned, turn_groups([far[j % 2, 2 * b + j // 2] for j in range(4)]))
        for part in range(2):
            for x in range(2):
                result[x, at, part * PLANE : (part + 1) * PLANE] = turned[2 * part + x]

    def fix_end(keep, order):
        def fix(at, own, near_by):
            done = [None] * 4
            for part in range(2):
                a = jnp.abs((2 * (2 * v + part) - 15).astype(f32)) * (0.9 / 15.0)
                first, second = [2 * part + x for x in order]
                one, two = near_by[second] * keep, near_by[first] * keep
                mark = [jnp.broadcast_to(own_marks[x, at, 0:1], (ROWS, PLANE)) for x in order]
                done[first] = stencil(own[first], one, two, a, mark[0])
                done[second] = stencil(own[second], own[first], one, a, mark[1])
            return done

        return fix

    @pl.when(up_end)
    def _():
        for n in range(CHUNKS):
            pltpu.make_async_copy(far.at[n], far.at[n], far_recv.at[n]).wait()
        fix = fix_end(jnp.where(group == 0, 0.0, 1.0), (0, 1))

        @pl.loop(0, GROUP // 2)
        def _(b):
            unpack(b, fix)

    @pl.when(down_end)
    def _():
        for n in range(CHUNKS):
            pltpu.make_async_copy(far.at[n], far.at[n], far_recv.at[n]).wait()
        fix = fix_end(jnp.where(group == total // TURNS - 1, 0.0, 1.0), (1, 0))

        @pl.loop(0, GROUP // 2)
        def _(b):
            unpack(b, fix)

    @pl.when(jnp.logical_not(jnp.logical_or(up_end, down_end)))
    def _():
        @pl.loop(0, GROUP // 2)
        def _(b):
            unpack(b, None)

    last = pltpu.make_async_copy(result, out, own_sem)
    last.start()
    for n in range(CHUNKS):
        for buf, sem in ((pack_in, in_send), (back, out_send)):
            pltpu.make_async_copy(buf.at[n, 0 : GROUP - 1], buf.at[n, 0 : GROUP - 1], sem.at[n]).wait()
        pltpu.make_async_copy(pack_far.at[n], pack_far.at[n], far_send.at[n]).wait()
    pltpu.make_async_copy(near.at[0:3], near.at[0:3], flag_send.at[0]).wait()
    last.wait()


def build(distribution, cell_flags, kernel_alpha, kernel_beta, kernel_loss, boundary_states):
    tile = (ROWS, PLANE)
    block = (VG * ROWS, PLANE)
    double = (2 * VG * ROWS, PLANE)
    anywhere = pl.BlockSpec(memory_space=pl.ANY)
    dma = pltpu.SemaphoreType.DMA

    def room(*dims):
        return pltpu.VMEM(dims + tile, f32)

    return pl.pallas_call(
        step_kernel,
        out_shape=jax.ShapeDtypeStruct(distribution.shape, f32),
        in_specs=[anywhere] * 7,
        out_specs=anywhere,
        scratch_shapes=[
            pltpu.VMEM(distribution.shape, f32),
            pltpu.VMEM((2, 128), jnp.int32),
            pltpu.VMEM((DIRS, VEL), f32),
            pltpu.VMEM((DIRS, VEL), f32),
            pltpu.VMEM((1, VEL), f32),
            pltpu.VMEM((2, VEL), f32),
            pltpu.VMEM((5, PLANE, PLANE), bf16),
            dma((7,)),
            room(CHUNKS, GROUP),
            room(CHUNKS, TURNS, PEERS),
            room(CHUNKS, PEERS // 2),
            room(CHUNKS, PEERS // 2),
            room(CHUNKS, PEERS, 2, 2),
            room(CHUNKS, PEERS),
            room(CHUNKS, GROUP),
            room(CHUNKS, TURNS, PEERS),
            room(CHUNKS, GROUP),
            pltpu.VMEM(distribution.shape, f32),
        ]
        + [pltpu.VMEM(block, f32)] * 3
        + [pltpu.VMEM(double, f32)] * 2
        + [pltpu.VMEM(block, f32)]
        + [
            pltpu.VMEM((FILTERS * VG, PLANE), f32),
            pltpu.VMEM((FILTERS, VG, 2, ROWS, 128), f32),
            pltpu.VMEM((TURNS, 2, 128), jnp.int32),
            pltpu.VMEM((2, 2, 128), jnp.int32),
            room(CHUNKS, 4),
            pltpu.VMEM((2, 128, 128), f32),
            dma((CHUNKS,)),
            dma((CHUNKS,)),
            dma((CHUNKS,)),
            dma((CHUNKS,)),
            dma((CHUNKS,)),
            dma((CHUNKS,)),
            dma((CHUNKS, 2)),
            dma((CHUNKS, 2)),
            dma((3,)),
            dma((3,)),
            dma(()),
        ],
        compiler_params=pltpu.CompilerParams(collective_id=0, has_side_effects=True),
    )(distribution, cell_flags, kernel_alpha, kernel_beta, kernel_loss.reshape(1, VEL), boundary_states, jnp.asarray(tables()))


def solution(mesh):
    return jax.shard_map(
        build,
        mesh=mesh,
        in_specs=(P("space", None, "vel"), P("space", None), P(), P(), P(), P()),
        out_specs=P("space", None, "vel"),
        check_vma=False,
    )
```

```python
import functools

import jax
import jax.numpy as jnp
import numpy as np
from jax import lax
from jax.experimental import pallas as pl
from jax.experimental.pallas import tpu as pltpu
from jax.sharding import PartitionSpec as P

VG = 16
PLANE = VG * VG
VEL = VG * PLANE
DIRS = 8
FILTERS = 2 * DIRS + 1
PEERS = 8
TURNS = 4
GROUP = TURNS * PEERS
ROWS = 8
CHUNKS = 2
GATE_TURN, GATE_PEER = 1, 2
MESH = pl.DeviceIdType.MESH
f32 = jnp.float32
bf16 = jnp.bfloat16


def half_modes():
    own = [((0, 0), (0, 8)), ((8, 0), (8, 8))]
    seen, pairs = set(), []
    for a in range(VG):
        for b in range(VG):
            twin = ((-a) % VG, (-b) % VG)
            if twin == (a, b) or twin in seen:
                continue
            seen.add((a, b))
            pairs.append((a, b))
    return own, pairs


def tables():
    own, pairs = half_modes()
    j, l = np.meshgrid(np.arange(VG), np.arange(VG), indexing="ij")
    j, l = j.reshape(-1), l.reshape(-1)

    def angle(mode):
        return ((mode[0] * j + mode[1] * l) % VG) * (2.0 * np.pi / VG)

    forward = np.zeros((PLANE, PLANE))
    inverse = np.zeros((PLANE, PLANE))
    pick = np.zeros((PLANE, PLANE))
    half = PLANE // 2
    for lane, (first, second) in enumerate(own):
        forward[:, lane] = np.cos(angle(first))
        forward[:, half + lane] = np.cos(angle(second))
        inverse[lane] = np.cos(angle(first))
        inverse[half + lane] = np.cos(angle(second))
        one, two = (first[0] * VG + first[1], second[0] * VG + second[1])
        pick[one, lane] = pick[two, lane] = 0.5
        pick[one, half + lane], pick[two, half + lane] = 0.5, -0.5
    for lane, mode in enumerate(pairs, start=len(own)):
        forward[:, lane] = np.cos(angle(mode))
        forward[:, half + lane] = -np.sin(angle(mode))
        inverse[lane] = 2.0 * np.cos(angle(mode))
        inverse[half + lane] = -2.0 * np.sin(angle(mode))
        pick[mode[0] * VG + mode[1], lane] = 1.0

    def parts(table):
        high = table.astype(np.float32).astype(bf16)
        low = (table - high.astype(np.float64)).astype(np.float32).astype(bf16)
        return [high, low]

    stack = parts(forward) + parts(inverse / VEL) + [pick.astype(bf16)]
    return np.stack(stack)


def times_root(re, im, power):
    power %= VG
    if power == 0:
        return re, im
    if power == 4:
        return im, -re
    c = float(np.cos(2.0 * np.pi * power / VG))
    s = float(np.sin(2.0 * np.pi * power / VG))
    if power == 2:
        return (re + im) * c, (im - re) * c
    if power == 6:
        return (im - re) * s, (re + im) * (-s)
    return re * c + im * s, im * c - re * s


def four_points(z):
    (ar, ai), (br, bi), (cr, ci), (dr, di) = z
    pr, pi_, mr, mi = ar + cr, ai + ci, ar - cr, ai - ci
    qr, qi, nr, ni = br + dr, bi + di, br - dr, bi - di
    return [(pr + qr, pi_ + qi), (mr + ni, mi - nr), (pr - qr, pi_ - qi), (mr - ni, mi + nr)]


def line_transform(z):
    mid = [four_points([z[4 * a + b] for a in range(4)]) for b in range(4)]
    out = [None] * VG
    for k in range(4):
        group = four_points([times_root(*mid[b][k], b * k) for b in range(4)])
        for m in range(4):
            out[k + 4 * m] = group[m]
    return out


def line_inverse(z):
    flipped = line_transform([(im, re) for re, im in z])
    return [(re, im) for im, re in flipped]


def split_two(x):
    high = x.astype(bf16)
    return high, (x - high.astype(f32)).astype(bf16)


def dot_three(x, high, low):
    x_high, x_low = split_two(x)
    dot = functools.partial(jnp.dot, preferred_element_type=f32)
    return dot(x_high, high) + (dot(x_low, high) + dot(x_high, low))


def row_ids(width):
    return lax.broadcasted_iota(jnp.int32, (ROWS, width), 0)


def roll(x, shift):
    return pltpu.roll(x, shift, 0)


def swap_halves(a, b):
    low = row_ids(a.shape[1]) < 4
    return jnp.where(low, a, roll(b, 4)), jnp.where(low, roll(a, 4), b)


def swap_pairs(a, b):
    low = row_ids(a.shape[1]) % 4 < 2
    return jnp.where(low, a, roll(b, 2)), jnp.where(low, roll(a, 6), b)


def turn_groups(tiles):
    a, b, c, d = tiles
    a, c = swap_halves(a, c)
    b, d = swap_halves(b, d)
    a, b = swap_pairs(a, b)
    c, d = swap_pairs(c, d)
    return [a, b, c, d]


def flag_tile(rows, offset):
    lanes = lax.broadcasted_iota(jnp.int32, (ROWS, 128), 1)
    ids = row_ids(128)
    wide = jnp.zeros((ROWS, 128), f32)
    for at, row in enumerate(rows):
        if row is not None:
            wide = jnp.where(ids // 2 == at, jnp.broadcast_to(row.astype(f32), (ROWS, 128)), wide)
    return jnp.sum(jnp.where(lanes == ids % 2 + offset, wide, 0.0), axis=1, keepdims=True)


def ghost(val, mark, low, high):
    return jnp.where(mark == 1.0, low, jnp.where(mark == 2.0, high, val))


def stencil(g, one, two, a, mark):
    second = (1.0 - 1.5 * a + 0.5 * a * a) * g + (2.0 * a - a * a) * one + (0.5 * a * a - 0.5 * a) * two
    return jnp.where(mark == 0.0, second, jnp.where(mark == 3.0, g - a * (g - one), g))


def transport(marks, states, tiles_of, halo_of, put, outer, inner):
    edge, mid = marks(1), marks(2)
    ids = row_ids(PLANE)

    def side(v, positive):
        tiles = tiles_of(v)
        outs = []
        for part in range(2):
            at = pl.ds(pl.multiple_of((2 * v + part) * PLANE, PLANE), PLANE)
            low, high = states[0:1, at], states[1:2, at]
            a = jnp.abs((2 * (2 * v + part) - 15).astype(f32)) * (0.9 / 15.0)
            e = ghost(tiles[part][0], edge, low, high)
            m = ghost(tiles[part][1], mid, low, high)
            new_e, new_m = None, None
            if inner:
                if positive:
                    one = jnp.where(ids < 2, roll(e, 6), roll(m, 2))
                    two = jnp.where(ids < 4, e, roll(m, 4))
                else:
                    one = jnp.where(ids < 6, roll(m, 6), roll(e, 2))
                    two = jnp.where(ids < 4, roll(m, 4), e)
                new_m = stencil(m, one, two, a, mid)
            if outer:
                if halo_of is None:
                    two = m
                else:
                    halo = halo_of(v, positive)
                    if positive == (part == 1):
                        halo = roll(halo, 4)
                    mark = marks(0) if positive else marks(3)
                    halo = ghost(jnp.where(mark == 4.0, 0.0, halo), mark, low, high)
                    two = jnp.where((ids < 4) == positive, halo, m)
                if positive:
                    one = jnp.where(ids % 4 < 2, roll(two, 6), roll(e, 2))
                else:
                    one = jnp.where(ids % 4 < 2, roll(e, 6), roll(two, 2))
                new_e = stencil(e, one, two, a, edge)
            outs.append((new_e, new_m, e))
        put(v, positive, outs)

    @pl.loop(0, 4)
    def _(v):
        side(v, False)

    @pl.loop(4, 8)
    def _(v):
        side(v, True)


def collide(filters, tab, moved, spec, modes, first, second, gain):
    half = PLANE // 2
    rows = VG * ROWS

    def piece(ref, k, base=0):
        at = base + k * ROWS
        return ref[at : at + ROWS, 0:half], ref[at : at + ROWS, half:PLANE]

    def put(ref, k, val, base=0):
        at = base + k * ROWS
        ref[at : at + ROWS, 0:half] = val[0]
        ref[at : at + ROWS, half:PLANE] = val[1]

    spec[...] = dot_three(moved[...], tab[0], tab[1])
    done = line_transform([piece(spec, k) for k in range(VG)])
    for k in range(VG):
        put(modes, k, done[k])

    def filtered(index, target, base):
        z = [piece(modes, k) for k in range(VG)]
        w = []
        for k in range(VG):
            near, far = filters[index, k, 0], filters[index, k, 1]
            twin = z[-k % VG]
            w.append((near * z[k][0] + far * twin[0], near * z[k][1] - far * twin[1]))
        done = line_inverse(w)
        for k in range(VG):
            put(target, k, done[k], base)

    def both(p, target):
        filtered(p, target, 0)
        filtered(p + DIRS, target, rows)

    def product(source):
        got = dot_three(source[...], tab[2], tab[3])
        return got[0:rows] * got[rows:]

    filtered(2 * DIRS, second, 0)
    both(0, first)
    loss = dot_three(second[0:rows, :], tab[2], tab[3])
    gain[...] = -(moved[...] * loss)

    @pl.loop(0, DIRS // 2 - 1)
    def _(h):
        both(2 * h + 1, second)
        gain[...] += product(first)
        both(2 * h + 2, first)
        gain[...] += product(second)

    both(DIRS - 1, second)
    gain[...] += product(first)
    gain[...] += product(second)


def step_kernel(
    dist_in, flags_in, alpha_in, beta_in, loss_in, states_in, tab_in, out,
    dist, flags, alpha, beta, loss, states, tab, load_sem,
    pack_in, recv, left1, right1, coll, pack_far, far, pack_out, back,
    moved, spec, modes, first, second, gain, packed, filters, near, edge, marks, own_marks,
    in_send, in_recv, out_send, out_recv, far_send, far_recv, halo_send, halo_recv, flag_send, flag_recv, gate_sem, ready_sem,
):
    s, v = lax.axis_index("space"), lax.axis_index("vel")
    total = lax.axis_size("space")
    group, turn = s // TURNS, s % TURNS
    upper = group % 2
    me = turn * PEERS + v

    def mirror(peer):
        return (peer + PEERS // 2) % PEERS

    def block_of(t, peer):
        return (peer + upper * (mirror(peer) - peer)) * TURNS + t

    def peer_at(q):
        return {"space": group * TURNS + q // PEERS, "vel": q % PEERS}

    right = {"space": (s + TURNS) % total, "vel": mirror(v)}
    left = {"space": (s + total - TURNS) % total, "vel": mirror(v)}
    mine = block_of(turn, v)

    loads = [
        pltpu.make_async_copy(src, dst, load_sem.at[i])
        for i, (src, dst) in enumerate(
            [(dist_in, dist), (flags_in, flags), (alpha_in, alpha), (beta_in, beta), (loss_in, loss), (states_in, states), (tab_in, tab)]
        )
    ]
    for copy in loads:
        copy.start()
    barrier = pltpu.get_barrier_semaphore()

    @pl.loop(1, GROUP)
    def _(d):
        pl.semaphore_signal(barrier, inc=1, device_id=peer_at((me + d) % GROUP), device_id_type=MESH)

    gate = jnp.logical_and(turn == GATE_TURN, v == GATE_PEER)

    def next_gate(semaphore):
        for step in (TURNS, total - TURNS):
            at = {"space": (s + step) % total, "vel": v}
            pl.semaphore_signal(semaphore, inc=1, device_id=at, device_id_type=MESH)

    @pl.when(gate)
    def _():
        next_gate(barrier)

    loads[0].wait()

    @pl.loop(0, GROUP // 2)
    def _(b):
        at = pl.ds(pl.multiple_of(b * ROWS, ROWS), ROWS)
        turned = turn_groups([dist[x, at, part * PLANE : (part + 1) * PLANE] for part in range(2) for x in range(2)])
        for j in range(4):
            pack_in[j % 2, 2 * b + j // 2] = turned[j]

    for copy in loads[1:]:
        copy.wait()
    pl.semaphore_wait(barrier, jnp.where(gate, GROUP + 1, GROUP - 1))

    def remote(src, dst, send, rec, at):
        return pltpu.make_async_remote_copy(
            src_ref=src, dst_ref=dst, send_sem=send, recv_sem=rec, device_id=at, device_id_type=MESH
        )

    for d in range(1, TURNS):
        at = {"space": group * TURNS + (turn + d) % TURNS, "vel": v}
        remote(flags, near.at[turn], flag_send.at[0], flag_recv.at[0], at).start()
    pltpu.make_async_copy(flags, near.at[turn], flag_recv.at[0]).start()

    for n in range(CHUNKS):

        @pl.loop(1, GROUP)
        def _(d):
            q = (me + d) % GROUP
            src = pack_in.at[n, block_of(q // PEERS, q % PEERS)]
            remote(src, recv.at[n, turn, v], in_send.at[n], in_recv.at[n], peer_at(q)).start()

        pltpu.make_async_copy(pack_in.at[n, mine], recv.at[n, turn, v], in_recv.at[n]).start()

    @pl.when(gate)
    def _():
        next_gate(gate_sem)
        pl.semaphore_wait(gate_sem, 2)

        @pl.loop(1, GROUP)
        def _(d):
            pl.semaphore_signal(ready_sem, inc=1, device_id=peer_at((me + d) % GROUP), device_id_type=MESH)

    def pick(rest):
        got = jnp.zeros(rest.shape, f32)
        for _ in range(3):
            one = rest.astype(bf16)
            rest = rest - one.astype(f32)
            got = got + jnp.dot(one, tab[4], preferred_element_type=f32)
        return got

    def by_line(ref):
        return jnp.concatenate([ref[:, k * PLANE : (k + 1) * PLANE] for k in range(VG)], 0)

    packed[0 : VG * DIRS, :] = pick(by_line(alpha))
    packed[VG * DIRS : 2 * VG * DIRS, :] = pick(by_line(beta))
    packed[2 * VG * DIRS :, :] = pick(by_line(loss))
    for k in range(VG):
        for f in range(FILTERS):
            at = 2 * VG * DIRS + k if f == 2 * DIRS else (f // DIRS) * VG * DIRS + k * DIRS + f % DIRS
            for part in range(2):
                row = packed[at : at + 1, part * 128 : (part + 1) * 128]
                filters[f, k, part] = jnp.broadcast_to(row, (ROWS, 128))

    pltpu.make_async_copy(near, near, flag_recv.at[0]).wait()
    @pl.when(jnp.logical_not(gate))
    def _():
        pl.semaphore_wait(ready_sem, 1)

    edges = [
        remote(near.at[3], edge.at[0], flag_send.at[1], flag_recv.at[1], right),
        remote(near.at[0], edge.at[1], flag_send.at[2], flag_recv.at[2], left),
    ]
    for copy in edges:
        copy.start()
    offset = mine * 4
    for n in range(CHUNKS):
        for at, pair in ((1, (0, 3)), (2, (1, 2))):
            rows = [near[pair[r // 2], r % 2 : r % 2 + 1, :] for r in range(4)]
            marks[n, at] = jnp.broadcast_to(flag_tile(rows, offset + 2 * n), (ROWS, PLANE))

    for x in range(2):
        wide = jnp.broadcast_to(flags[x : x + 1, :].astype(f32), (ROWS, 128))
        lanes = lax.broadcasted_iota(jnp.int32, (ROWS, 128), 1)
        for b in range(GROUP // 2):
            column = jnp.sum(jnp.where(lanes == row_ids(128) + b * ROWS, wide, 0.0), axis=1, keepdims=True)
            own_marks[x, b * ROWS : (b + 1) * ROWS, :] = jnp.broadcast_to(column, (ROWS, 128))

    def exchange(at, ups, downs, ups_dst, downs_dst):
        one = remote(ups, ups_dst, halo_send.at[at, 0], halo_recv.at[at, 0], right)
        two = remote(downs, downs_dst, halo_send.at[at, 1], halo_recv.at[at, 1], left)
        one.start()
        two.start()
        return [one, two]

    def settle(copies):
        for copy in copies:
            copy.wait()

    def begin(n):
        pltpu.make_async_copy(recv.at[n], recv.at[n], in_recv.at[n]).wait()
        return exchange(n, recv.at[n, 3, 4:8], recv.at[n, 0, 0:4], left1.at[n], right1.at[n])

    def work(n, which):
        def tiles_of(u):
            one = swap_halves(recv[n, 0, u], recv[n, 3, u])
            two = swap_halves(recv[n, 1, u], recv[n, 2, u])
            return [(one[part], two[part]) for part in range(2)]

        def halo_of(u, positive):
            return left1[n, u - 4] if positive else right1[n, u]

        def put_moved(u, positive, outs):
            for part in range(2):
                at = pl.multiple_of((2 * u + part) * ROWS, ROWS)
                moved[pl.ds(at, ROWS), :] = outs[part][which]

        transport(lambda r: marks[n, r], states, tiles_of, halo_of, put_moved, which == 0, which == 1)
        collide(filters, tab, moved, spec, modes, first, second, gain)
        for u in range(PEERS):
            pair = []
            for part in range(2):
                at = (2 * u + part) * ROWS
                pair.append(moved[at : at + ROWS, :] + 0.5 * gain[at : at + ROWS, :])
                coll[n, u, part, which] = pair[part]

    def give(n, t, u):
        q = t * PEERS + u

        @pl.when(q != me)
        def _():
            remote(pack_out.at[n, t, u], back.at[n, mine], out_send.at[n], out_recv.at[n], peer_at(q)).start()

        @pl.when(q == me)
        def _():
            pltpu.make_async_copy(pack_out.at[n, t, u], back.at[n, mine], out_recv.at[n]).start()

    def finish_mid(n):
        def tiles_of(u):
            return [(coll[n, u, part, 1], coll[n, u, part, 1]) for part in range(2)]

        def put_done(u, positive, outs):
            one, two = swap_halves(outs[0][1], outs[1][1])
            if positive:
                pack_out[n, 2, u] = two
            else:
                pack_out[n, 1, u] = one

        transport(lambda r: marks[n, r], states, tiles_of, None, put_done, False, True)

        @pl.loop(0, PEERS)
        def _(d):
            u = (v + 1 + d) % PEERS
            give(n, 1 + u // 4, u)

    def finish(n):
        def tiles_of(u):
            return [(coll[n, u, part, 0], coll[n, u, part, 1]) for part in range(2)]

        def put_done(u, positive, outs):
            one, two = swap_halves(outs[0][1], outs[1][1])
            ends = swap_halves(outs[0][0], outs[1][0])
            raw = swap_halves(outs[0][2], outs[1][2])
            if positive:
                pack_out[n, 1, u] = one
                pack_out[n, 3, u] = ends[1]
                pack_out[n, 0, u] = raw[0]
                pack_far[n, u] = raw[1]
            else:
                pack_out[n, 2, u] = two
                pack_out[n, 0, u] = ends[0]
                pack_out[n, 3, u] = raw[1]
                pack_far[n, u] = raw[0]

        transport(lambda r: marks[n, r], states, tiles_of, None, put_done, True, True)

        @pl.loop(0, PEERS)
        def _(d):
            u = (v + d) % PEERS
            at = (s - turn + total + TURNS * (2 * (u // 4) - 1)) % total + 3 * (1 - u // 4)
            remote(pack_far.at[n, u], far.at[n, mine], far_send.at[n], far_recv.at[n], {"space": at, "vel": u}).start()

        @pl.loop(0, 3 * PEERS)
        def _(d):
            u = (v + 1 + d) % PEERS
            k = (turn + d // PEERS) % 3
            give(n, jnp.where(k == 2, 2 - u // 4, 3 * k), u)

    one1 = begin(0)
    work(0, 1)
    finish_mid(0)
    settle(edges)
    for n in range(CHUNKS):
        lefts = flag_tile([edge[0, 0:1, :], edge[0, 1:2, :], None, None], offset + 2 * n)
        rights = flag_tile([None, None, edge[1, 0:1, :], edge[1, 1:2, :]], offset + 2 * n)
        marks[n, 0] = jnp.broadcast_to(jnp.where(group == 0, 4.0, lefts), (ROWS, PLANE))
        marks[n, 3] = jnp.broadcast_to(jnp.where(group == total // TURNS - 1, 4.0, rights), (ROWS, PLANE))
    two1 = begin(1)
    settle(one1)
    work(0, 0)
    finish(0)
    work(1, 1)
    finish_mid(1)
    settle(two1)
    work(1, 0)
    finish(1)
    for n in range(CHUNKS):
        pltpu.make_async_copy(back.at[n], back.at[n], out_recv.at[n]).wait()
    up_end = jnp.logical_and(turn == 0, v >= PEERS // 2)
    down_end = jnp.logical_and(turn == TURNS - 1, v < PEERS // 2)

    def unpack(b, fix):
        at = pl.ds(pl.multiple_of(b * ROWS, ROWS), ROWS)
        turned = turn_groups([back[j % 2, 2 * b + j // 2] for j in range(4)])
        if fix is not None:
            turned = fix(at, turned, turn_groups([far[j % 2, 2 * b + j // 2] for j in range(4)]))
        for part in range(2):
            for x in range(2):
                out[x, at, part * PLANE : (part + 1) * PLANE] = turned[2 * part + x]

    def fix_end(keep, order):
        def fix(at, own, near_by):
            done = [None] * 4
            for part in range(2):
                a = jnp.abs((2 * (2 * v + part) - 15).astype(f32)) * (0.9 / 15.0)
                first, second = [2 * part + x for x in order]
                one, two = near_by[second] * keep, near_by[first] * keep
                mark = [jnp.broadcast_to(own_marks[x, at, 0:1], (ROWS, PLANE)) for x in order]
                done[first] = stencil(own[first], one, two, a, mark[0])
                done[second] = stencil(own[second], own[first], one, a, mark[1])
            return done

        return fix

    @pl.when(up_end)
    def _():
        for n in range(CHUNKS):
            pltpu.make_async_copy(far.at[n], far.at[n], far_recv.at[n]).wait()
        fix = fix_end(jnp.where(group == 0, 0.0, 1.0), (0, 1))

        @pl.loop(0, GROUP // 2)
        def _(b):
            unpack(b, fix)

    @pl.when(down_end)
    def _():
        for n in range(CHUNKS):
            pltpu.make_async_copy(far.at[n], far.at[n], far_recv.at[n]).wait()
        fix = fix_end(jnp.where(group == total // TURNS - 1, 0.0, 1.0), (1, 0))

        @pl.loop(0, GROUP // 2)
        def _(b):
            unpack(b, fix)

    @pl.when(jnp.logical_not(jnp.logical_or(up_end, down_end)))
    def _():
        @pl.loop(0, GROUP // 2)
        def _(b):
            unpack(b, None)

    for n in range(CHUNKS):
        for buf, sem in ((pack_in, in_send), (back, out_send)):
            pltpu.make_async_copy(buf.at[n, 0 : GROUP - 1], buf.at[n, 0 : GROUP - 1], sem.at[n]).wait()
        pltpu.make_async_copy(pack_far.at[n], pack_far.at[n], far_send.at[n]).wait()
    pltpu.make_async_copy(near.at[0:3], near.at[0:3], flag_send.at[0]).wait()


def build(distribution, cell_flags, kernel_alpha, kernel_beta, kernel_loss, boundary_states):
    tile = (ROWS, PLANE)
    block = (VG * ROWS, PLANE)
    double = (2 * VG * ROWS, PLANE)
    anywhere = pl.BlockSpec(memory_space=pl.ANY)
    dma = pltpu.SemaphoreType.DMA

    def room(*dims):
        return pltpu.VMEM(dims + tile, f32)

    return pl.pallas_call(
        step_kernel,
        out_shape=jax.ShapeDtypeStruct(distribution.shape, f32),
        in_specs=[anywhere] * 7,
        out_specs=pl.BlockSpec(memory_space=pltpu.VMEM),
        scratch_shapes=[
            pltpu.VMEM(distribution.shape, f32),
            pltpu.VMEM((2, 128), jnp.int32),
            pltpu.VMEM((DIRS, VEL), f32),
            pltpu.VMEM((DIRS, VEL), f32),
            pltpu.VMEM((1, VEL), f32),
            pltpu.VMEM((2, VEL), f32),
            pltpu.VMEM((5, PLANE, PLANE), bf16),
            dma((7,)),
            room(CHUNKS, GROUP),
            room(CHUNKS, TURNS, PEERS),
            room(CHUNKS, PEERS // 2),
            room(CHUNKS, PEERS // 2),
            room(CHUNKS, PEERS, 2, 2),
            room(CHUNKS, PEERS),
            room(CHUNKS, GROUP),
            room(CHUNKS, TURNS, PEERS),
            room(CHUNKS, GROUP),
        ]
        + [pltpu.VMEM(block, f32)] * 3
        + [pltpu.VMEM(double, f32)] * 2
        + [pltpu.VMEM(block, f32)]
        + [
            pltpu.VMEM((FILTERS * VG, PLANE), f32),
            pltpu.VMEM((FILTERS, VG, 2, ROWS, 128), f32),
            pltpu.VMEM((TURNS, 2, 128), jnp.int32),
            pltpu.VMEM((2, 2, 128), jnp.int32),
            room(CHUNKS, 4),
            pltpu.VMEM((2, 128, 128), f32),
            dma((CHUNKS,)),
            dma((CHUNKS,)),
            dma((CHUNKS,)),
            dma((CHUNKS,)),
            dma((CHUNKS,)),
            dma((CHUNKS,)),
            dma((CHUNKS, 2)),
            dma((CHUNKS, 2)),
            dma((3,)),
            dma((3,)),
            pltpu.SemaphoreType.REGULAR,
            pltpu.SemaphoreType.REGULAR,
        ],
        compiler_params=pltpu.CompilerParams(collective_id=0, has_side_effects=True),
    )(distribution, cell_flags, kernel_alpha, kernel_beta, kernel_loss.reshape(1, VEL), boundary_states, jnp.asarray(tables()))


def solution(mesh):
    return jax.shard_map(
        build,
        mesh=mesh,
        in_specs=(P("space", None, "vel"), P("space", None), P(), P(), P(), P()),
        out_specs=P("space", None, "vel"),
        check_vma=False,
    )
```

```python
import functools

import jax
import jax.numpy as jnp
import numpy as np
from jax import lax
from jax.experimental import pallas as pl
from jax.experimental.pallas import tpu as pltpu
from jax.sharding import PartitionSpec as P

VG = 16
PLANE = VG * VG
VEL = VG * PLANE
DIRS = 8
FILTERS = 2 * DIRS + 1
PEERS = 8
TURNS = 4
GROUP = TURNS * PEERS
ROWS = 8
CHUNKS = 2
GATE_TURN, GATE_PEER = 1, 2
MESH = pl.DeviceIdType.MESH
f32 = jnp.float32
bf16 = jnp.bfloat16


def half_modes():
    own = [((0, 0), (0, 8)), ((8, 0), (8, 8))]
    seen, pairs = set(), []
    for a in range(VG):
        for b in range(VG):
            twin = ((-a) % VG, (-b) % VG)
            if twin == (a, b) or twin in seen:
                continue
            seen.add((a, b))
            pairs.append((a, b))
    return own, pairs


def tables():
    own, pairs = half_modes()
    j, l = np.meshgrid(np.arange(VG), np.arange(VG), indexing="ij")
    j, l = j.reshape(-1), l.reshape(-1)

    def angle(mode):
        return ((mode[0] * j + mode[1] * l) % VG) * (2.0 * np.pi / VG)

    forward = np.zeros((PLANE, PLANE))
    inverse = np.zeros((PLANE, PLANE))
    pick = np.zeros((PLANE, PLANE))
    half = PLANE // 2
    for lane, (first, second) in enumerate(own):
        forward[:, lane] = np.cos(angle(first))
        forward[:, half + lane] = np.cos(angle(second))
        inverse[lane] = np.cos(angle(first))
        inverse[half + lane] = np.cos(angle(second))
        one, two = (first[0] * VG + first[1], second[0] * VG + second[1])
        pick[one, lane] = pick[two, lane] = 0.5
        pick[one, half + lane], pick[two, half + lane] = 0.5, -0.5
    for lane, mode in enumerate(pairs, start=len(own)):
        forward[:, lane] = np.cos(angle(mode))
        forward[:, half + lane] = -np.sin(angle(mode))
        inverse[lane] = 2.0 * np.cos(angle(mode))
        inverse[half + lane] = -2.0 * np.sin(angle(mode))
        pick[mode[0] * VG + mode[1], lane] = 1.0

    def parts(table):
        high = table.astype(np.float32).astype(bf16)
        low = (table - high.astype(np.float64)).astype(np.float32).astype(bf16)
        return [high, low]

    stack = parts(forward) + parts(inverse / VEL) + [pick.astype(bf16)]
    return np.stack(stack)


def times_root(re, im, power):
    power %= VG
    if power == 0:
        return re, im
    if power == 4:
        return im, -re
    c = float(np.cos(2.0 * np.pi * power / VG))
    s = float(np.sin(2.0 * np.pi * power / VG))
    if power == 2:
        return (re + im) * c, (im - re) * c
    if power == 6:
        return (im - re) * s, (re + im) * (-s)
    return re * c + im * s, im * c - re * s


def four_points(z):
    (ar, ai), (br, bi), (cr, ci), (dr, di) = z
    pr, pi_, mr, mi = ar + cr, ai + ci, ar - cr, ai - ci
    qr, qi, nr, ni = br + dr, bi + di, br - dr, bi - di
    return [(pr + qr, pi_ + qi), (mr + ni, mi - nr), (pr - qr, pi_ - qi), (mr - ni, mi + nr)]


def line_transform(z):
    mid = [four_points([z[4 * a + b] for a in range(4)]) for b in range(4)]
    out = [None] * VG
    for k in range(4):
        group = four_points([times_root(*mid[b][k], b * k) for b in range(4)])
        for m in range(4):
            out[k + 4 * m] = group[m]
    return out


def line_inverse(z):
    flipped = line_transform([(im, re) for re, im in z])
    return [(re, im) for im, re in flipped]


def split_two(x):
    high = x.astype(bf16)
    return high, (x - high.astype(f32)).astype(bf16)


def dot_three(x, high, low):
    x_high, x_low = split_two(x)
    dot = functools.partial(jnp.dot, preferred_element_type=f32)
    return dot(x_high, high) + (dot(x_low, high) + dot(x_high, low))


def row_ids(width):
    return lax.broadcasted_iota(jnp.int32, (ROWS, width), 0)


def roll(x, shift):
    return pltpu.roll(x, shift, 0)


def swap_halves(a, b):
    low = row_ids(a.shape[1]) < 4
    return jnp.where(low, a, roll(b, 4)), jnp.where(low, roll(a, 4), b)


def swap_pairs(a, b):
    low = row_ids(a.shape[1]) % 4 < 2
    return jnp.where(low, a, roll(b, 2)), jnp.where(low, roll(a, 6), b)


def turn_groups(tiles):
    a, b, c, d = tiles
    a, c = swap_halves(a, c)
    b, d = swap_halves(b, d)
    a, b = swap_pairs(a, b)
    c, d = swap_pairs(c, d)
    return [a, b, c, d]


def flag_tile(rows, offset):
    lanes = lax.broadcasted_iota(jnp.int32, (ROWS, 128), 1)
    ids = row_ids(128)
    wide = jnp.zeros((ROWS, 128), f32)
    for at, row in enumerate(rows):
        if row is not None:
            wide = jnp.where(ids // 2 == at, jnp.broadcast_to(row.astype(f32), (ROWS, 128)), wide)
    return jnp.sum(jnp.where(lanes == ids % 2 + offset, wide, 0.0), axis=1, keepdims=True)


def ghost(val, mark, low, high):
    return jnp.where(mark == 1.0, low, jnp.where(mark == 2.0, high, val))


def stencil(g, one, two, a, mark):
    second = (1.0 - 1.5 * a + 0.5 * a * a) * g + (2.0 * a - a * a) * one + (0.5 * a * a - 0.5 * a) * two
    return jnp.where(mark == 0.0, second, jnp.where(mark == 3.0, g - a * (g - one), g))


def transport(marks, states, tiles_of, halo_of, put, outer, inner):
    edge, mid = marks(1), marks(2)
    ids = row_ids(PLANE)

    def side(v, positive):
        tiles = tiles_of(v)
        outs = []
        for part in range(2):
            at = pl.ds(pl.multiple_of((2 * v + part) * PLANE, PLANE), PLANE)
            low, high = states[0:1, at], states[1:2, at]
            a = jnp.abs((2 * (2 * v + part) - 15).astype(f32)) * (0.9 / 15.0)
            e = ghost(tiles[part][0], edge, low, high)
            m = ghost(tiles[part][1], mid, low, high)
            new_e, new_m = None, None
            if inner:
                if positive:
                    one = jnp.where(ids < 2, roll(e, 6), roll(m, 2))
                    two = jnp.where(ids < 4, e, roll(m, 4))
                else:
                    one = jnp.where(ids < 6, roll(m, 6), roll(e, 2))
                    two = jnp.where(ids < 4, roll(m, 4), e)
                new_m = stencil(m, one, two, a, mid)
            if outer:
                if halo_of is None:
                    two = m
                else:
                    halo = halo_of(v, positive)
                    if positive == (part == 1):
                        halo = roll(halo, 4)
                    mark = marks(0) if positive else marks(3)
                    halo = ghost(jnp.where(mark == 4.0, 0.0, halo), mark, low, high)
                    two = jnp.where((ids < 4) == positive, halo, m)
                if positive:
                    one = jnp.where(ids % 4 < 2, roll(two, 6), roll(e, 2))
                else:
                    one = jnp.where(ids % 4 < 2, roll(e, 6), roll(two, 2))
                new_e = stencil(e, one, two, a, edge)
            outs.append((new_e, new_m))
        put(v, positive, outs)

    @pl.loop(0, 4)
    def _(v):
        side(v, False)

    @pl.loop(4, 8)
    def _(v):
        side(v, True)


def collide(filters, tab, moved, spec, modes, first, second, gain):
    half = PLANE // 2
    rows = VG * ROWS

    def piece(ref, k, base=0):
        at = base + k * ROWS
        return ref[at : at + ROWS, 0:half], ref[at : at + ROWS, half:PLANE]

    def put(ref, k, val, base=0):
        at = base + k * ROWS
        ref[at : at + ROWS, 0:half] = val[0]
        ref[at : at + ROWS, half:PLANE] = val[1]

    spec[...] = dot_three(moved[...], tab[0], tab[1])
    done = line_transform([piece(spec, k) for k in range(VG)])
    for k in range(VG):
        put(modes, k, done[k])

    def filtered(index, target, base):
        z = [piece(modes, k) for k in range(VG)]
        w = []
        for k in range(VG):
            near, far = filters[index, k, 0], filters[index, k, 1]
            twin = z[-k % VG]
            w.append((near * z[k][0] + far * twin[0], near * z[k][1] - far * twin[1]))
        done = line_inverse(w)
        for k in range(VG):
            put(target, k, done[k], base)

    def both(p, target):
        filtered(p, target, 0)
        filtered(p + DIRS, target, rows)

    def product(source):
        got = dot_three(source[...], tab[2], tab[3])
        return got[0:rows] * got[rows:]

    filtered(2 * DIRS, second, 0)
    both(0, first)
    loss = dot_three(second[0:rows, :], tab[2], tab[3])
    gain[...] = -(moved[...] * loss)

    @pl.loop(0, DIRS // 2 - 1)
    def _(h):
        both(2 * h + 1, second)
        gain[...] += product(first)
        both(2 * h + 2, first)
        gain[...] += product(second)

    both(DIRS - 1, second)
    gain[...] += product(first)
    gain[...] += product(second)


def step_kernel(
    dist_in, flags_in, alpha_in, beta_in, loss_in, states_in, tab_in, out,
    dist, flags, alpha, beta, loss, states, tab, load_sem,
    pack_in, recv, left1, right1, coll, edge_out, left2, right2, pack_out, back,
    moved, spec, modes, first, second, gain, packed, filters, near, edge, marks,
    in_send, in_recv, out_send, out_recv, halo_send, halo_recv, flag_send, flag_recv, gate_sem, ready_sem,
):
    s, v = lax.axis_index("space"), lax.axis_index("vel")
    total = lax.axis_size("space")
    group, turn = s // TURNS, s % TURNS
    upper = group % 2
    me = turn * PEERS + v

    def mirror(peer):
        return (peer + PEERS // 2) % PEERS

    def block_of(t, peer):
        return (peer + upper * (mirror(peer) - peer)) * TURNS + t

    def peer_at(q):
        return {"space": group * TURNS + q // PEERS, "vel": q % PEERS}

    right = {"space": (s + TURNS) % total, "vel": mirror(v)}
    left = {"space": (s + total - TURNS) % total, "vel": mirror(v)}
    mine = block_of(turn, v)

    loads = [
        pltpu.make_async_copy(src, dst, load_sem.at[i])
        for i, (src, dst) in enumerate(
            [(dist_in, dist), (flags_in, flags), (alpha_in, alpha), (beta_in, beta), (loss_in, loss), (states_in, states), (tab_in, tab)]
        )
    ]
    loads[0].start()
    barrier = pltpu.get_barrier_semaphore()

    @pl.loop(1, GROUP)
    def _(d):
        pl.semaphore_signal(barrier, inc=1, device_id=peer_at((me + d) % GROUP), device_id_type=MESH)

    gate = jnp.logical_and(turn == GATE_TURN, v == GATE_PEER)

    def next_gate(semaphore):
        for step in (TURNS, total - TURNS):
            at = {"space": (s + step) % total, "vel": v}
            pl.semaphore_signal(semaphore, inc=1, device_id=at, device_id_type=MESH)

    @pl.when(gate)
    def _():
        next_gate(barrier)

    loads[0].wait()
    for copy in loads[1:]:
        copy.start()

    @pl.loop(0, GROUP // 2)
    def _(b):
        at = pl.ds(pl.multiple_of(b * ROWS, ROWS), ROWS)
        turned = turn_groups([dist[x, at, part * PLANE : (part + 1) * PLANE] for part in range(2) for x in range(2)])
        for j in range(4):
            pack_in[j % 2, 2 * b + j // 2] = turned[j]

    loads[1].wait()
    pl.semaphore_wait(barrier, jnp.where(gate, GROUP + 1, GROUP - 1))

    def remote(src, dst, send, rec, at):
        return pltpu.make_async_remote_copy(
            src_ref=src, dst_ref=dst, send_sem=send, recv_sem=rec, device_id=at, device_id_type=MESH
        )

    for d in range(1, TURNS):
        at = {"space": group * TURNS + (turn + d) % TURNS, "vel": v}
        remote(flags, near.at[turn], flag_send.at[0], flag_recv.at[0], at).start()
    pltpu.make_async_copy(flags, near.at[turn], flag_recv.at[0]).start()

    upward = jnp.logical_and(turn == TURNS - 1, v >= PEERS // 2)
    downward = jnp.logical_and(turn == 0, v < PEERS // 2)
    kind = jnp.where(upward, 0, jnp.where(downward, 1, 2))
    for n in range(CHUNKS):

        @pl.loop(1, GROUP)
        def _(d):
            q = (me + d) % GROUP
            src = pack_in.at[n, block_of(q // PEERS, q % PEERS)]
            remote(src, recv.at[n, turn, v], in_send.at[n], in_recv.at[n, kind], peer_at(q)).start()

        pltpu.make_async_copy(pack_in.at[n, mine], recv.at[n, turn, v], in_recv.at[n, kind]).start()

    @pl.when(gate)
    def _():
        next_gate(gate_sem)
        pl.semaphore_wait(gate_sem, 2)

        @pl.loop(1, GROUP)
        def _(d):
            pl.semaphore_signal(ready_sem, inc=1, device_id=peer_at((me + d) % GROUP), device_id_type=MESH)

    for copy in loads[2:]:
        copy.wait()

    def pick(rest):
        got = jnp.zeros(rest.shape, f32)
        for _ in range(3):
            one = rest.astype(bf16)
            rest = rest - one.astype(f32)
            got = got + jnp.dot(one, tab[4], preferred_element_type=f32)
        return got

    def by_line(ref):
        return jnp.concatenate([ref[:, k * PLANE : (k + 1) * PLANE] for k in range(VG)], 0)

    packed[0 : VG * DIRS, :] = pick(by_line(alpha))
    packed[VG * DIRS : 2 * VG * DIRS, :] = pick(by_line(beta))
    packed[2 * VG * DIRS :, :] = pick(by_line(loss))
    for k in range(VG):
        for f in range(FILTERS):
            at = 2 * VG * DIRS + k if f == 2 * DIRS else (f // DIRS) * VG * DIRS + k * DIRS + f % DIRS
            for part in range(2):
                row = packed[at : at + 1, part * 128 : (part + 1) * 128]
                filters[f, k, part] = jnp.broadcast_to(row, (ROWS, 128))

    pltpu.make_async_copy(near, near, flag_recv.at[0]).wait()
    @pl.when(jnp.logical_not(gate))
    def _():
        pl.semaphore_wait(ready_sem, 1)

    edges = [
        remote(near.at[3], edge.at[0], flag_send.at[1], flag_recv.at[1], right),
        remote(near.at[0], edge.at[1], flag_send.at[2], flag_recv.at[2], left),
    ]
    for copy in edges:
        copy.start()
    offset = mine * 4
    for n in range(CHUNKS):
        for at, pair in ((1, (0, 3)), (2, (1, 2))):
            rows = [near[pair[r // 2], r % 2 : r % 2 + 1, :] for r in range(4)]
            marks[n, at] = jnp.broadcast_to(flag_tile(rows, offset + 2 * n), (ROWS, PLANE))

    def settle(copies):
        for copy in copies:
            copy.wait()

    def exchange(at, ends, before):
        copies = []
        for way, (src, dst, to) in enumerate(ends):
            before(way, src)
            copies.append(remote(src, dst, halo_send.at[at, way], halo_recv.at[at, way], to))
            copies[way].start()
        return copies

    def begin(n):
        def landed(way, src):
            pltpu.make_async_copy(src, src, in_recv.at[n, way]).wait()

        ends = ((recv.at[n, 3, 4:8], left1.at[n], right), (recv.at[n, 0, 0:4], right1.at[n], left))
        return exchange(n, ends, landed)

    def pass_on(n):
        ends = ((edge_out.at[n, 0], left2.at[n], right), (edge_out.at[n, 1], right2.at[n], left))
        return exchange(CHUNKS + n, ends, lambda way, src: None)

    def rest_of(n):
        rest = recv.at[n, 0:3]
        pltpu.make_async_copy(rest, rest, in_recv.at[n, 2]).wait()

    def work(n, which):
        def tiles_of(u):
            one = swap_halves(recv[n, 0, u], recv[n, 3, u])
            two = swap_halves(recv[n, 1, u], recv[n, 2, u])
            return [(one[part], two[part]) for part in range(2)]

        def halo_of(u, positive):
            return left1[n, u - 4] if positive else right1[n, u]

        def put_moved(u, positive, outs):
            for part in range(2):
                at = pl.multiple_of((2 * u + part) * ROWS, ROWS)
                moved[pl.ds(at, ROWS), :] = outs[part][which]

        transport(lambda r: marks[n, r], states, tiles_of, halo_of, put_moved, which == 0, which == 1)
        collide(filters, tab, moved, spec, modes, first, second, gain)
        for u in range(PEERS):
            pair = []
            for part in range(2):
                at = (2 * u + part) * ROWS
                pair.append(moved[at : at + ROWS, :] + 0.5 * gain[at : at + ROWS, :])
                coll[n, u, part, which] = pair[part]
            if which == 0 and u < 4:
                edge_out[n, 1, u] = swap_halves(*pair)[0]
            if which == 0 and u >= 4:
                edge_out[n, 0, u - 4] = swap_halves(*pair)[1]

    def give(n, t, u):
        q = t * PEERS + u

        @pl.when(q != me)
        def _():
            remote(pack_out.at[n, t, u], back.at[n, mine], out_send.at[n], out_recv.at[n], peer_at(q)).start()

        @pl.when(q == me)
        def _():
            pltpu.make_async_copy(pack_out.at[n, t, u], back.at[n, mine], out_recv.at[n]).start()

    def finish_mid(n):
        def tiles_of(u):
            return [(coll[n, u, part, 1], coll[n, u, part, 1]) for part in range(2)]

        def put_done(u, positive, outs):
            one, two = swap_halves(outs[0][1], outs[1][1])
            if positive:
                pack_out[n, 2, u] = two
            else:
                pack_out[n, 1, u] = one

        transport(lambda r: marks[n, r], states, tiles_of, None, put_done, False, True)

        @pl.loop(0, PEERS)
        def _(d):
            u = (v + 1 + d) % PEERS
            give(n, 1 + u // 4, u)

    def tiles_done(n):
        def tiles_of(u):
            return [(coll[n, u, part, 0], coll[n, u, part, 1]) for part in range(2)]

        return tiles_of

    def finish_most(n):
        def put_done(u, positive, outs):
            one, two = swap_halves(outs[0][1], outs[1][1])
            ends = swap_halves(outs[0][0], outs[1][0])
            if positive:
                pack_out[n, 1, u] = one
                pack_out[n, 3, u] = ends[1]
            else:
                pack_out[n, 2, u] = two
                pack_out[n, 0, u] = ends[0]

        transport(lambda r: marks[n, r], states, tiles_done(n), None, put_done, True, True)

        @pl.loop(0, 2 * PEERS)
        def _(d):
            u = (v + 1 + d) % PEERS
            k = (turn + d // PEERS) % 2
            give(n, (2 - u // 4) * k + (3 * (u // 4)) * (1 - k), u)

    def finish_rest(n):
        def halo_of(u, positive):
            return left2[n, u - 4] if positive else right2[n, u]

        def put_done(u, positive, outs):
            ends = swap_halves(outs[0][0], outs[1][0])
            if positive:
                pack_out[n, 0, u] = ends[0]
            else:
                pack_out[n, 3, u] = ends[1]

        transport(lambda r: marks[n, r], states, tiles_done(n), halo_of, put_done, True, False)

        @pl.loop(0, PEERS)
        def _(d):
            u = (v + 1 + d) % PEERS
            give(n, 3 - 3 * (u // 4), u)

    one1 = begin(0)
    rest_of(0)
    work(0, 1)
    finish_mid(0)
    settle(edges)
    for n in range(CHUNKS):
        lefts = flag_tile([edge[0, 0:1, :], edge[0, 1:2, :], None, None], offset + 2 * n)
        rights = flag_tile([None, None, edge[1, 0:1, :], edge[1, 1:2, :]], offset + 2 * n)
        marks[n, 0] = jnp.broadcast_to(jnp.where(group == 0, 4.0, lefts), (ROWS, PLANE))
        marks[n, 3] = jnp.broadcast_to(jnp.where(group == total // TURNS - 1, 4.0, rights), (ROWS, PLANE))
    two1 = begin(1)
    rest_of(1)
    work(1, 1)
    finish_mid(1)
    settle(one1)
    work(0, 0)
    one2 = pass_on(0)
    finish_most(0)
    settle(two1)
    work(1, 0)
    two2 = pass_on(1)
    finish_most(1)
    settle(one2)
    finish_rest(0)
    settle(two2)
    finish_rest(1)
    for n in range(CHUNKS):
        pltpu.make_async_copy(back.at[n], back.at[n], out_recv.at[n]).wait()

    @pl.loop(0, GROUP // 2)
    def _(b):
        at = pl.ds(pl.multiple_of(b * ROWS, ROWS), ROWS)
        turned = turn_groups([back[j % 2, 2 * b + j // 2] for j in range(4)])
        for part in range(2):
            for x in range(2):
                out[x, at, part * PLANE : (part + 1) * PLANE] = turned[2 * part + x]

    for n in range(CHUNKS):
        for buf, sem in ((pack_in, in_send), (back, out_send)):
            pltpu.make_async_copy(buf.at[n, 0 : GROUP - 1], buf.at[n, 0 : GROUP - 1], sem.at[n]).wait()
    pltpu.make_async_copy(near.at[0:3], near.at[0:3], flag_send.at[0]).wait()


def build(distribution, cell_flags, kernel_alpha, kernel_beta, kernel_loss, boundary_states):
    tile = (ROWS, PLANE)
    block = (VG * ROWS, PLANE)
    double = (2 * VG * ROWS, PLANE)
    anywhere = pl.BlockSpec(memory_space=pl.ANY)
    dma = pltpu.SemaphoreType.DMA

    def room(*dims):
        return pltpu.VMEM(dims + tile, f32)

    return pl.pallas_call(
        step_kernel,
        out_shape=jax.ShapeDtypeStruct(distribution.shape, f32),
        in_specs=[anywhere] * 7,
        out_specs=pl.BlockSpec(memory_space=pltpu.VMEM),
        scratch_shapes=[
            pltpu.VMEM(distribution.shape, f32),
            pltpu.VMEM((2, 128), jnp.int32),
            pltpu.VMEM((DIRS, VEL), f32),
            pltpu.VMEM((DIRS, VEL), f32),
            pltpu.VMEM((1, VEL), f32),
            pltpu.VMEM((2, VEL), f32),
            pltpu.VMEM((5, PLANE, PLANE), bf16),
            dma((7,)),
            room(CHUNKS, GROUP),
            room(CHUNKS, TURNS, PEERS),
            room(CHUNKS, PEERS // 2),
            room(CHUNKS, PEERS // 2),
            room(CHUNKS, PEERS, 2, 2),
            room(CHUNKS, 2, PEERS // 2),
            room(CHUNKS, PEERS // 2),
            room(CHUNKS, PEERS // 2),
            room(CHUNKS, TURNS, PEERS),
            room(CHUNKS, GROUP),
        ]
        + [pltpu.VMEM(block, f32)] * 3
        + [pltpu.VMEM(double, f32)] * 2
        + [pltpu.VMEM(block, f32)]
        + [
            pltpu.VMEM((FILTERS * VG, PLANE), f32),
            pltpu.VMEM((FILTERS, VG, 2, ROWS, 128), f32),
            pltpu.VMEM((TURNS, 2, 128), jnp.int32),
            pltpu.VMEM((2, 2, 128), jnp.int32),
            room(CHUNKS, 4),
            dma((CHUNKS,)),
            dma((CHUNKS, 3)),
            dma((CHUNKS,)),
            dma((CHUNKS,)),
            dma((2 * CHUNKS, 2)),
            dma((2 * CHUNKS, 2)),
            dma((3,)),
            dma((3,)),
            pltpu.SemaphoreType.REGULAR,
            pltpu.SemaphoreType.REGULAR,
        ],
        compiler_params=pltpu.CompilerParams(collective_id=0, has_side_effects=True),
    )(distribution, cell_flags, kernel_alpha, kernel_beta, kernel_loss.reshape(1, VEL), boundary_states, jnp.asarray(tables()))


def solution(mesh):
    return jax.shard_map(
        build,
        mesh=mesh,
        in_specs=(P("space", None, "vel"), P("space", None), P(), P(), P(), P()),
        out_specs=P("space", None, "vel"),
        check_vma=False,
    )
```

```python
import functools

import jax
import jax.numpy as jnp
import numpy as np
from jax import lax
from jax.experimental import pallas as pl
from jax.experimental.pallas import tpu as pltpu
from jax.sharding import PartitionSpec as P

VG = 16
PLANE = VG * VG
VEL = VG * PLANE
DIRS = 8
FILTERS = 2 * DIRS + 1
PEERS = 8
TURNS = 4
GROUP = TURNS * PEERS
ROWS = 8
CHUNKS = 2
GATE_TURN, GATE_PEER = 1, 2
MESH = pl.DeviceIdType.MESH
f32 = jnp.float32
bf16 = jnp.bfloat16


def half_modes():
    own = [((0, 0), (0, 8)), ((8, 0), (8, 8))]
    seen, pairs = set(), []
    for a in range(VG):
        for b in range(VG):
            twin = ((-a) % VG, (-b) % VG)
            if twin == (a, b) or twin in seen:
                continue
            seen.add((a, b))
            pairs.append((a, b))
    return own, pairs


def tables():
    own, pairs = half_modes()
    j, l = np.meshgrid(np.arange(VG), np.arange(VG), indexing="ij")
    j, l = j.reshape(-1), l.reshape(-1)

    def angle(mode):
        return ((mode[0] * j + mode[1] * l) % VG) * (2.0 * np.pi / VG)

    forward = np.zeros((PLANE, PLANE))
    inverse = np.zeros((PLANE, PLANE))
    pick = np.zeros((PLANE, PLANE))
    half = PLANE // 2
    for lane, (first, second) in enumerate(own):
        forward[:, lane] = np.cos(angle(first))
        forward[:, half + lane] = np.cos(angle(second))
        inverse[lane] = np.cos(angle(first))
        inverse[half + lane] = np.cos(angle(second))
        one, two = (first[0] * VG + first[1], second[0] * VG + second[1])
        pick[one, lane] = pick[two, lane] = 0.5
        pick[one, half + lane], pick[two, half + lane] = 0.5, -0.5
    for lane, mode in enumerate(pairs, start=len(own)):
        forward[:, lane] = np.cos(angle(mode))
        forward[:, half + lane] = -np.sin(angle(mode))
        inverse[lane] = 2.0 * np.cos(angle(mode))
        inverse[half + lane] = -2.0 * np.sin(angle(mode))
        pick[mode[0] * VG + mode[1], lane] = 1.0

    def parts(table):
        high = table.astype(np.float32).astype(bf16)
        low = (table - high.astype(np.float64)).astype(np.float32).astype(bf16)
        return [high, low]

    stack = parts(forward) + parts(inverse / VEL) + [pick.astype(bf16)]
    return np.stack(stack)


def times_root(re, im, power):
    power %= VG
    if power == 0:
        return re, im
    if power == 4:
        return im, -re
    c = float(np.cos(2.0 * np.pi * power / VG))
    s = float(np.sin(2.0 * np.pi * power / VG))
    if power == 2:
        return (re + im) * c, (im - re) * c
    if power == 6:
        return (im - re) * s, (re + im) * (-s)
    return re * c + im * s, im * c - re * s


def four_points(z):
    (ar, ai), (br, bi), (cr, ci), (dr, di) = z
    pr, pi_, mr, mi = ar + cr, ai + ci, ar - cr, ai - ci
    qr, qi, nr, ni = br + dr, bi + di, br - dr, bi - di
    return [(pr + qr, pi_ + qi), (mr + ni, mi - nr), (pr - qr, pi_ - qi), (mr - ni, mi + nr)]


def line_transform(z):
    mid = [four_points([z[4 * a + b] for a in range(4)]) for b in range(4)]
    out = [None] * VG
    for k in range(4):
        group = four_points([times_root(*mid[b][k], b * k) for b in range(4)])
        for m in range(4):
            out[k + 4 * m] = group[m]
    return out


def line_inverse(z):
    flipped = line_transform([(im, re) for re, im in z])
    return [(re, im) for im, re in flipped]


def split_two(x):
    high = x.astype(bf16)
    return high, (x - high.astype(f32)).astype(bf16)


def dot_three(x, high, low):
    x_high, x_low = split_two(x)
    dot = functools.partial(jnp.dot, preferred_element_type=f32)
    return dot(x_high, high) + (dot(x_low, high) + dot(x_high, low))


def row_ids(width):
    return lax.broadcasted_iota(jnp.int32, (ROWS, width), 0)


def roll(x, shift):
    return pltpu.roll(x, shift, 0)


def swap_halves(a, b):
    low = row_ids(a.shape[1]) < 4
    return jnp.where(low, a, roll(b, 4)), jnp.where(low, roll(a, 4), b)


def swap_pairs(a, b):
    low = row_ids(a.shape[1]) % 4 < 2
    return jnp.where(low, a, roll(b, 2)), jnp.where(low, roll(a, 6), b)


def turn_groups(tiles):
    a, b, c, d = tiles
    a, c = swap_halves(a, c)
    b, d = swap_halves(b, d)
    a, b = swap_pairs(a, b)
    c, d = swap_pairs(c, d)
    return [a, b, c, d]


def flag_tile(rows, offset):
    lanes = lax.broadcasted_iota(jnp.int32, (ROWS, 128), 1)
    ids = row_ids(128)
    wide = jnp.zeros((ROWS, 128), f32)
    for at, row in enumerate(rows):
        if row is not None:
            wide = jnp.where(ids // 2 == at, jnp.broadcast_to(row.astype(f32), (ROWS, 128)), wide)
    return jnp.sum(jnp.where(lanes == ids % 2 + offset, wide, 0.0), axis=1, keepdims=True)


def ghost(val, mark, low, high):
    return jnp.where(mark == 1.0, low, jnp.where(mark == 2.0, high, val))


def stencil(g, one, two, a, mark):
    second = (1.0 - 1.5 * a + 0.5 * a * a) * g + (2.0 * a - a * a) * one + (0.5 * a * a - 0.5 * a) * two
    return jnp.where(mark == 0.0, second, jnp.where(mark == 3.0, g - a * (g - one), g))


def transport(marks, states, tiles_of, halo_of, put, outer, inner):
    edge, mid = marks(1), marks(2)
    ids = row_ids(PLANE)

    def side(v, positive):
        tiles = tiles_of(v)
        outs = []
        for part in range(2):
            at = pl.ds(pl.multiple_of((2 * v + part) * PLANE, PLANE), PLANE)
            low, high = states[0:1, at], states[1:2, at]
            a = jnp.abs((2 * (2 * v + part) - 15).astype(f32)) * (0.9 / 15.0)
            e = ghost(tiles[part][0], edge, low, high)
            m = ghost(tiles[part][1], mid, low, high)
            new_e, new_m = None, None
            if inner:
                if positive:
                    one = jnp.where(ids < 2, roll(e, 6), roll(m, 2))
                    two = jnp.where(ids < 4, e, roll(m, 4))
                else:
                    one = jnp.where(ids < 6, roll(m, 6), roll(e, 2))
                    two = jnp.where(ids < 4, roll(m, 4), e)
                new_m = stencil(m, one, two, a, mid)
            if outer:
                if halo_of is None:
                    two = m
                else:
                    halo = halo_of(v, positive)
                    if positive == (part == 1):
                        halo = roll(halo, 4)
                    mark = marks(0) if positive else marks(3)
                    halo = ghost(jnp.where(mark == 4.0, 0.0, halo), mark, low, high)
                    two = jnp.where((ids < 4) == positive, halo, m)
                if positive:
                    one = jnp.where(ids % 4 < 2, roll(two, 6), roll(e, 2))
                else:
                    one = jnp.where(ids % 4 < 2, roll(e, 6), roll(two, 2))
                new_e = stencil(e, one, two, a, edge)
            outs.append((new_e, new_m))
        put(v, positive, outs)

    @pl.loop(0, 4)
    def _(v):
        side(v, False)

    @pl.loop(4, 8)
    def _(v):
        side(v, True)


def collide(filters, tab, moved, spec, modes, first, second, gain):
    half = PLANE // 2
    rows = VG * ROWS

    def piece(ref, k, base=0):
        at = base + k * ROWS
        return ref[at : at + ROWS, 0:half], ref[at : at + ROWS, half:PLANE]

    def put(ref, k, val, base=0):
        at = base + k * ROWS
        ref[at : at + ROWS, 0:half] = val[0]
        ref[at : at + ROWS, half:PLANE] = val[1]

    spec[...] = dot_three(moved[...], tab[0], tab[1])
    done = line_transform([piece(spec, k) for k in range(VG)])
    for k in range(VG):
        put(modes, k, done[k])

    def filtered(index, target, base):
        def weighed(k):
            near, far = filters[index, k, 0], filters[index, k, 1]
            (re, im), (twin_re, twin_im) = piece(modes, k), piece(modes, -k % VG)
            return im * near - far * twin_im, re * near + far * twin_re

        for b in range(4):
            group = four_points([weighed(4 * a + b) for a in range(4)])
            for k in range(4):
                put(target, 4 * b + k, times_root(*group[k], b * k), base)
        for k in range(4):
            group = four_points([piece(target, 4 * b + k, base) for b in range(4)])
            for m in range(4):
                re, im = group[m]
                put(target, k + 4 * m, (im, re), base)

    def both(p, target):
        filtered(p, target, 0)
        filtered(p + DIRS, target, rows)

    def product(source):
        got = dot_three(source[...], tab[2], tab[3])
        return got[0:rows] * got[rows:]

    filtered(2 * DIRS, second, 0)
    both(0, first)
    loss = dot_three(second[0:rows, :], tab[2], tab[3])
    gain[...] = -(moved[...] * loss)

    @pl.loop(0, DIRS // 2 - 1)
    def _(h):
        both(2 * h + 1, second)
        gain[...] += product(first)
        both(2 * h + 2, first)
        gain[...] += product(second)

    both(DIRS - 1, second)
    gain[...] += product(first)
    gain[...] += product(second)


def step_kernel(
    dist_in, flags_in, alpha_in, beta_in, loss_in, states_in, tab_in, out,
    dist, flags, alpha, beta, loss, states, tab, load_sem,
    pack_in, recv, left1, right1, coll, edge_out, left2, right2, pack_out, back,
    moved, spec, modes, first, second, gain, packed, filters, near, edge, marks,
    in_send, in_recv, out_send, out_recv, halo_send, halo_recv, flag_send, flag_recv, gate_sem, ready_sem,
):
    s, v = lax.axis_index("space"), lax.axis_index("vel")
    total = lax.axis_size("space")
    group, turn = s // TURNS, s % TURNS
    upper = group % 2
    me = turn * PEERS + v

    def mirror(peer):
        return (peer + PEERS // 2) % PEERS

    def block_of(t, peer):
        return (peer + upper * (mirror(peer) - peer)) * TURNS + t

    def peer_at(q):
        return {"space": group * TURNS + q // PEERS, "vel": q % PEERS}

    right = {"space": (s + TURNS) % total, "vel": mirror(v)}
    left = {"space": (s + total - TURNS) % total, "vel": mirror(v)}
    mine = block_of(turn, v)

    loads = [
        pltpu.make_async_copy(src, dst, load_sem.at[i])
        for i, (src, dst) in enumerate(
            [(dist_in, dist), (flags_in, flags), (alpha_in, alpha), (beta_in, beta), (loss_in, loss), (states_in, states), (tab_in, tab)]
        )
    ]
    loads[0].start()
    barrier = pltpu.get_barrier_semaphore()

    @pl.loop(1, GROUP)
    def _(d):
        pl.semaphore_signal(barrier, inc=1, device_id=peer_at((me + d) % GROUP), device_id_type=MESH)

    gate = jnp.logical_and(turn == GATE_TURN, v == GATE_PEER)

    def next_gate(semaphore):
        for step in (TURNS, total - TURNS):
            at = {"space": (s + step) % total, "vel": v}
            pl.semaphore_signal(semaphore, inc=1, device_id=at, device_id_type=MESH)

    @pl.when(gate)
    def _():
        next_gate(barrier)

    loads[0].wait()
    for copy in loads[1:]:
        copy.start()

    @pl.loop(0, GROUP // 2)
    def _(b):
        at = pl.ds(pl.multiple_of(b * ROWS, ROWS), ROWS)
        turned = turn_groups([dist[x, at, part * PLANE : (part + 1) * PLANE] for part in range(2) for x in range(2)])
        for j in range(4):
            pack_in[j % 2, 2 * b + j // 2] = turned[j]

    loads[1].wait()
    pl.semaphore_wait(barrier, jnp.where(gate, GROUP + 1, GROUP - 1))

    def remote(src, dst, send, rec, at):
        return pltpu.make_async_remote_copy(
            src_ref=src, dst_ref=dst, send_sem=send, recv_sem=rec, device_id=at, device_id_type=MESH
        )

    for d in range(1, TURNS):
        at = {"space": group * TURNS + (turn + d) % TURNS, "vel": v}
        remote(flags, near.at[turn], flag_send.at[0], flag_recv.at[0], at).start()
    pltpu.make_async_copy(flags, near.at[turn], flag_recv.at[0]).start()

    upward = jnp.logical_and(turn == TURNS - 1, v >= PEERS // 2)
    downward = jnp.logical_and(turn == 0, v < PEERS // 2)
    kind = jnp.where(upward, 0, jnp.where(downward, 1, 2))
    for n in range(CHUNKS):

        @pl.loop(1, GROUP)
        def _(d):
            q = (me + d) % GROUP
            src = pack_in.at[n, block_of(q // PEERS, q % PEERS)]
            remote(src, recv.at[n, turn, v], in_send.at[n], in_recv.at[n, kind], peer_at(q)).start()

        pltpu.make_async_copy(pack_in.at[n, mine], recv.at[n, turn, v], in_recv.at[n, kind]).start()

    @pl.when(gate)
    def _():
        next_gate(gate_sem)
        pl.semaphore_wait(gate_sem, 2)

        @pl.loop(1, GROUP)
        def _(d):
            pl.semaphore_signal(ready_sem, inc=1, device_id=peer_at((me + d) % GROUP), device_id_type=MESH)

    for copy in loads[2:]:
        copy.wait()

    def pick(rest):
        got = jnp.zeros(rest.shape, f32)
        for _ in range(3):
            one = rest.astype(bf16)
            rest = rest - one.astype(f32)
            got = got + jnp.dot(one, tab[4], preferred_element_type=f32)
        return got

    def by_line(ref):
        return jnp.concatenate([ref[:, k * PLANE : (k + 1) * PLANE] for k in range(VG)], 0)

    packed[0 : VG * DIRS, :] = pick(by_line(alpha))
    packed[VG * DIRS : 2 * VG * DIRS, :] = pick(by_line(beta))
    packed[2 * VG * DIRS :, :] = pick(by_line(loss))
    for k in range(VG):
        for f in range(FILTERS):
            at = 2 * VG * DIRS + k if f == 2 * DIRS else (f // DIRS) * VG * DIRS + k * DIRS + f % DIRS
            for part in range(2):
                row = packed[at : at + 1, part * 128 : (part + 1) * 128]
                filters[f, k, part] = jnp.broadcast_to(row, (ROWS, 128))

    pltpu.make_async_copy(near, near, flag_recv.at[0]).wait()
    @pl.when(jnp.logical_not(gate))
    def _():
        pl.semaphore_wait(ready_sem, 1)

    edges = [
        remote(near.at[3], edge.at[0], flag_send.at[1], flag_recv.at[1], right),
        remote(near.at[0], edge.at[1], flag_send.at[2], flag_recv.at[2], left),
    ]
    for copy in edges:
        copy.start()
    offset = mine * 4
    for n in range(CHUNKS):
        for at, pair in ((1, (0, 3)), (2, (1, 2))):
            rows = [near[pair[r // 2], r % 2 : r % 2 + 1, :] for r in range(4)]
            marks[n, at] = jnp.broadcast_to(flag_tile(rows, offset + 2 * n), (ROWS, PLANE))

    def settle(copies):
        for copy in copies:
            copy.wait()

    def exchange(at, ends, before):
        copies = []
        for way, (src, dst, to) in enumerate(ends):
            before(way, src)
            copies.append(remote(src, dst, halo_send.at[at, way], halo_recv.at[at, way], to))
            copies[way].start()
        return copies

    def begin(n):
        def landed(way, src):
            pltpu.make_async_copy(src, src, in_recv.at[n, way]).wait()

        ends = ((recv.at[n, 3, 4:8], left1.at[n], right), (recv.at[n, 0, 0:4], right1.at[n], left))
        return exchange(n, ends, landed)

    def pass_on(n):
        ends = ((edge_out.at[n, 0], left2.at[n], right), (edge_out.at[n, 1], right2.at[n], left))
        return exchange(CHUNKS + n, ends, lambda way, src: None)

    def rest_of(n):
        rest = recv.at[n, 0:3]
        pltpu.make_async_copy(rest, rest, in_recv.at[n, 2]).wait()

    def work(n, which):
        def tiles_of(u):
            one = swap_halves(recv[n, 0, u], recv[n, 3, u])
            two = swap_halves(recv[n, 1, u], recv[n, 2, u])
            return [(one[part], two[part]) for part in range(2)]

        def halo_of(u, positive):
            return left1[n, u - 4] if positive else right1[n, u]

        def put_moved(u, positive, outs):
            for part in range(2):
                at = pl.multiple_of((2 * u + part) * ROWS, ROWS)
                moved[pl.ds(at, ROWS), :] = outs[part][which]

        transport(lambda r: marks[n, r], states, tiles_of, halo_of, put_moved, which == 0, which == 1)
        collide(filters, tab, moved, spec, modes, first, second, gain)
        for u in range(PEERS):
            pair = []
            for part in range(2):
                at = (2 * u + part) * ROWS
                pair.append(moved[at : at + ROWS, :] + 0.5 * gain[at : at + ROWS, :])
                coll[n, u, part, which] = pair[part]
            if which == 0 and u < 4:
                edge_out[n, 1, u] = swap_halves(*pair)[0]
            if which == 0 and u >= 4:
                edge_out[n, 0, u - 4] = swap_halves(*pair)[1]

    def give(n, t, u):
        q = t * PEERS + u

        @pl.when(q != me)
        def _():
            remote(pack_out.at[n, t, u], back.at[n, mine], out_send.at[n], out_recv.at[n], peer_at(q)).start()

        @pl.when(q == me)
        def _():
            pltpu.make_async_copy(pack_out.at[n, t, u], back.at[n, mine], out_recv.at[n]).start()

    def finish_mid(n):
        def tiles_of(u):
            return [(coll[n, u, part, 1], coll[n, u, part, 1]) for part in range(2)]

        def put_done(u, positive, outs):
            one, two = swap_halves(outs[0][1], outs[1][1])
            if positive:
                pack_out[n, 2, u] = two
            else:
                pack_out[n, 1, u] = one

        transport(lambda r: marks[n, r], states, tiles_of, None, put_done, False, True)

        @pl.loop(0, PEERS)
        def _(d):
            u = (v + 1 + d) % PEERS
            give(n, 1 + u // 4, u)

    def tiles_done(n):
        def tiles_of(u):
            return [(coll[n, u, part, 0], coll[n, u, part, 1]) for part in range(2)]

        return tiles_of

    def finish_most(n):
        def put_done(u, positive, outs):
            one, two = swap_halves(outs[0][1], outs[1][1])
            ends = swap_halves(outs[0][0], outs[1][0])
            if positive:
                pack_out[n, 1, u] = one
                pack_out[n, 3, u] = ends[1]
            else:
                pack_out[n, 2, u] = two
                pack_out[n, 0, u] = ends[0]

        transport(lambda r: marks[n, r], states, tiles_done(n), None, put_done, True, True)

        @pl.loop(0, 2 * PEERS)
        def _(d):
            u = (v + 1 + d) % PEERS
            k = (turn + d // PEERS) % 2
            give(n, (2 - u // 4) * k + (3 * (u // 4)) * (1 - k), u)

    def finish_rest(n):
        def halo_of(u, positive):
            return left2[n, u - 4] if positive else right2[n, u]

        def put_done(u, positive, outs):
            ends = swap_halves(outs[0][0], outs[1][0])
            if positive:
                pack_out[n, 0, u] = ends[0]
            else:
                pack_out[n, 3, u] = ends[1]

        transport(lambda r: marks[n, r], states, tiles_done(n), halo_of, put_done, True, False)

        @pl.loop(0, PEERS)
        def _(d):
            u = (v + 1 + d) % PEERS
            give(n, 3 - 3 * (u // 4), u)

    one1 = begin(0)
    rest_of(0)
    work(0, 1)
    finish_mid(0)
    settle(edges)
    for n in range(CHUNKS):
        lefts = flag_tile([edge[0, 0:1, :], edge[0, 1:2, :], None, None], offset + 2 * n)
        rights = flag_tile([None, None, edge[1, 0:1, :], edge[1, 1:2, :]], offset + 2 * n)
        marks[n, 0] = jnp.broadcast_to(jnp.where(group == 0, 4.0, lefts), (ROWS, PLANE))
        marks[n, 3] = jnp.broadcast_to(jnp.where(group == total // TURNS - 1, 4.0, rights), (ROWS, PLANE))
    two1 = begin(1)
    rest_of(1)
    work(1, 1)
    finish_mid(1)
    settle(one1)
    work(0, 0)
    one2 = pass_on(0)
    finish_most(0)
    settle(two1)
    work(1, 0)
    two2 = pass_on(1)
    finish_most(1)
    settle(one2)
    finish_rest(0)
    settle(two2)
    finish_rest(1)
    for n in range(CHUNKS):
        pltpu.make_async_copy(back.at[n], back.at[n], out_recv.at[n]).wait()

    @pl.loop(0, GROUP // 2)
    def _(b):
        at = pl.ds(pl.multiple_of(b * ROWS, ROWS), ROWS)
        turned = turn_groups([back[j % 2, 2 * b + j // 2] for j in range(4)])
        for part in range(2):
            for x in range(2):
                out[x, at, part * PLANE : (part + 1) * PLANE] = turned[2 * part + x]

    for n in range(CHUNKS):
        for buf, sem in ((pack_in, in_send), (back, out_send)):
            pltpu.make_async_copy(buf.at[n, 0 : GROUP - 1], buf.at[n, 0 : GROUP - 1], sem.at[n]).wait()
    pltpu.make_async_copy(near.at[0:3], near.at[0:3], flag_send.at[0]).wait()


def build(distribution, cell_flags, kernel_alpha, kernel_beta, kernel_loss, boundary_states):
    tile = (ROWS, PLANE)
    block = (VG * ROWS, PLANE)
    double = (2 * VG * ROWS, PLANE)
    anywhere = pl.BlockSpec(memory_space=pl.ANY)
    dma = pltpu.SemaphoreType.DMA

    def room(*dims):
        return pltpu.VMEM(dims + tile, f32)

    return pl.pallas_call(
        step_kernel,
        out_shape=jax.ShapeDtypeStruct(distribution.shape, f32),
        in_specs=[anywhere] * 7,
        out_specs=pl.BlockSpec(memory_space=pltpu.VMEM),
        scratch_shapes=[
            pltpu.VMEM(distribution.shape, f32),
            pltpu.VMEM((2, 128), jnp.int32),
            pltpu.VMEM((DIRS, VEL), f32),
            pltpu.VMEM((DIRS, VEL), f32),
            pltpu.VMEM((1, VEL), f32),
            pltpu.VMEM((2, VEL), f32),
            pltpu.VMEM((5, PLANE, PLANE), bf16),
            dma((7,)),
            room(CHUNKS, GROUP),
            room(CHUNKS, TURNS, PEERS),
            room(CHUNKS, PEERS // 2),
            room(CHUNKS, PEERS // 2),
            room(CHUNKS, PEERS, 2, 2),
            room(CHUNKS, 2, PEERS // 2),
            room(CHUNKS, PEERS // 2),
            room(CHUNKS, PEERS // 2),
            room(CHUNKS, TURNS, PEERS),
            room(CHUNKS, GROUP),
        ]
        + [pltpu.VMEM(block, f32)] * 3
        + [pltpu.VMEM(double, f32)] * 2
        + [pltpu.VMEM(block, f32)]
        + [
            pltpu.VMEM((FILTERS * VG, PLANE), f32),
            pltpu.VMEM((FILTERS, VG, 2, ROWS, 128), f32),
            pltpu.VMEM((TURNS, 2, 128), jnp.int32),
            pltpu.VMEM((2, 2, 128), jnp.int32),
            room(CHUNKS, 4),
            dma((CHUNKS,)),
            dma((CHUNKS, 3)),
            dma((CHUNKS,)),
            dma((CHUNKS,)),
            dma((2 * CHUNKS, 2)),
            dma((2 * CHUNKS, 2)),
            dma((3,)),
            dma((3,)),
            pltpu.SemaphoreType.REGULAR,
            pltpu.SemaphoreType.REGULAR,
        ],
        compiler_params=pltpu.CompilerParams(collective_id=0, has_side_effects=True),
    )(distribution, cell_flags, kernel_alpha, kernel_beta, kernel_loss.reshape(1, VEL), boundary_states, jnp.asarray(tables()))


def solution(mesh):
    return jax.shard_map(
        build,
        mesh=mesh,
        in_specs=(P("space", None, "vel"), P("space", None), P(), P(), P(), P()),
        out_specs=P("space", None, "vel"),
        check_vma=False,
    )
```

```python
import functools

import jax
import jax.numpy as jnp
import numpy as np
from jax import lax
from jax.experimental import pallas as pl
from jax.experimental.pallas import tpu as pltpu
from jax.sharding import PartitionSpec as P

VG = 16
PLANE = VG * VG
VEL = VG * PLANE
DIRS = 8
FILTERS = 2 * DIRS + 1
PEERS = 8
TURNS = 4
GROUP = TURNS * PEERS
ROWS = 8
CHUNKS = 2
GATE_TURN, GATE_PEER = 1, 2
MESH = pl.DeviceIdType.MESH
f32 = jnp.float32
bf16 = jnp.bfloat16


def half_modes():
    own = [((0, 0), (0, 8)), ((8, 0), (8, 8))]
    seen, pairs = set(), []
    for a in range(VG):
        for b in range(VG):
            twin = ((-a) % VG, (-b) % VG)
            if twin == (a, b) or twin in seen:
                continue
            seen.add((a, b))
            pairs.append((a, b))
    return own, pairs


def tables():
    own, pairs = half_modes()
    j, l = np.meshgrid(np.arange(VG), np.arange(VG), indexing="ij")
    j, l = j.reshape(-1), l.reshape(-1)

    def angle(mode):
        return ((mode[0] * j + mode[1] * l) % VG) * (2.0 * np.pi / VG)

    forward = np.zeros((PLANE, PLANE))
    inverse = np.zeros((PLANE, PLANE))
    pick = np.zeros((PLANE, PLANE))
    half = PLANE // 2
    for lane, (first, second) in enumerate(own):
        forward[:, lane] = np.cos(angle(first))
        forward[:, half + lane] = np.cos(angle(second))
        inverse[lane] = np.cos(angle(first))
        inverse[half + lane] = np.cos(angle(second))
        one, two = (first[0] * VG + first[1], second[0] * VG + second[1])
        pick[one, lane] = pick[two, lane] = 0.5
        pick[one, half + lane], pick[two, half + lane] = 0.5, -0.5
    for lane, mode in enumerate(pairs, start=len(own)):
        forward[:, lane] = np.cos(angle(mode))
        forward[:, half + lane] = -np.sin(angle(mode))
        inverse[lane] = 2.0 * np.cos(angle(mode))
        inverse[half + lane] = -2.0 * np.sin(angle(mode))
        pick[mode[0] * VG + mode[1], lane] = 1.0

    def parts(table):
        high = table.astype(np.float32).astype(bf16)
        low = (table - high.astype(np.float64)).astype(np.float32).astype(bf16)
        return [high, low]

    stack = parts(forward) + parts(inverse / VEL) + [pick.astype(bf16)]
    return np.stack(stack)


def times_root(re, im, power):
    power %= VG
    if power == 0:
        return re, im
    if power == 4:
        return im, -re
    c = float(np.cos(2.0 * np.pi * power / VG))
    s = float(np.sin(2.0 * np.pi * power / VG))
    if power == 2:
        return (re + im) * c, (im - re) * c
    if power == 6:
        return (im - re) * s, (re + im) * (-s)
    return re * c + im * s, im * c - re * s


def four_points(z):
    (ar, ai), (br, bi), (cr, ci), (dr, di) = z
    pr, pi_, mr, mi = ar + cr, ai + ci, ar - cr, ai - ci
    qr, qi, nr, ni = br + dr, bi + di, br - dr, bi - di
    return [(pr + qr, pi_ + qi), (mr + ni, mi - nr), (pr - qr, pi_ - qi), (mr - ni, mi + nr)]


def line_transform(z):
    mid = [four_points([z[4 * a + b] for a in range(4)]) for b in range(4)]
    out = [None] * VG
    for k in range(4):
        group = four_points([times_root(*mid[b][k], b * k) for b in range(4)])
        for m in range(4):
            out[k + 4 * m] = group[m]
    return out


def line_inverse(z):
    flipped = line_transform([(im, re) for re, im in z])
    return [(re, im) for im, re in flipped]


def split_two(x):
    high = x.astype(bf16)
    return high, (x - high.astype(f32)).astype(bf16)


def dot_three(x, high, low):
    x_high, x_low = split_two(x)
    dot = functools.partial(jnp.dot, preferred_element_type=f32)
    return dot(x_high, high) + (dot(x_low, high) + dot(x_high, low))


def row_ids(width):
    return lax.broadcasted_iota(jnp.int32, (ROWS, width), 0)


def roll(x, shift):
    return pltpu.roll(x, shift, 0)


def swap_halves(a, b):
    low = row_ids(a.shape[1]) < 4
    return jnp.where(low, a, roll(b, 4)), jnp.where(low, roll(a, 4), b)


def swap_pairs(a, b):
    low = row_ids(a.shape[1]) % 4 < 2
    return jnp.where(low, a, roll(b, 2)), jnp.where(low, roll(a, 6), b)


def turn_groups(tiles):
    a, b, c, d = tiles
    a, c = swap_halves(a, c)
    b, d = swap_halves(b, d)
    a, b = swap_pairs(a, b)
    c, d = swap_pairs(c, d)
    return [a, b, c, d]


def flag_tile(rows, offset):
    lanes = lax.broadcasted_iota(jnp.int32, (ROWS, 128), 1)
    ids = row_ids(128)
    wide = jnp.zeros((ROWS, 128), f32)
    for at, row in enumerate(rows):
        if row is not None:
            wide = jnp.where(ids // 2 == at, jnp.broadcast_to(row.astype(f32), (ROWS, 128)), wide)
    return jnp.sum(jnp.where(lanes == ids % 2 + offset, wide, 0.0), axis=1, keepdims=True)


def ghost(val, mark, low, high):
    return jnp.where(mark == 1.0, low, jnp.where(mark == 2.0, high, val))


def stencil(g, one, two, a, mark):
    second = (1.0 - 1.5 * a + 0.5 * a * a) * g + (2.0 * a - a * a) * one + (0.5 * a * a - 0.5 * a) * two
    return jnp.where(mark == 0.0, second, jnp.where(mark == 3.0, g - a * (g - one), g))


def transport(marks, states, tiles_of, halo_of, put, outer, inner):
    edge, mid = marks(1), marks(2)
    ids = row_ids(PLANE)

    def side(v, positive):
        tiles = tiles_of(v)
        outs = []
        for part in range(2):
            at = pl.ds(pl.multiple_of((2 * v + part) * PLANE, PLANE), PLANE)
            low, high = states[0:1, at], states[1:2, at]
            a = jnp.abs((2 * (2 * v + part) - 15).astype(f32)) * (0.9 / 15.0)
            e = ghost(tiles[part][0], edge, low, high)
            m = ghost(tiles[part][1], mid, low, high)
            new_e, new_m = None, None
            if inner:
                if positive:
                    one = jnp.where(ids < 2, roll(e, 6), roll(m, 2))
                    two = jnp.where(ids < 4, e, roll(m, 4))
                else:
                    one = jnp.where(ids < 6, roll(m, 6), roll(e, 2))
                    two = jnp.where(ids < 4, roll(m, 4), e)
                new_m = stencil(m, one, two, a, mid)
            if outer:
                if halo_of is None:
                    two = m
                else:
                    halo = halo_of(v, positive)
                    if positive == (part == 1):
                        halo = roll(halo, 4)
                    mark = marks(0) if positive else marks(3)
                    halo = ghost(jnp.where(mark == 4.0, 0.0, halo), mark, low, high)
                    two = jnp.where((ids < 4) == positive, halo, m)
                if positive:
                    one = jnp.where(ids % 4 < 2, roll(two, 6), roll(e, 2))
                else:
                    one = jnp.where(ids % 4 < 2, roll(e, 6), roll(two, 2))
                new_e = stencil(e, one, two, a, edge)
            outs.append((new_e, new_m))
        put(v, positive, outs)

    @pl.loop(0, 4)
    def _(v):
        side(v, False)

    @pl.loop(4, 8)
    def _(v):
        side(v, True)


def collide(filters, tab, moved, spec, modes, first, second, gain):
    half = PLANE // 2
    rows = VG * ROWS

    def piece(ref, k, base=0):
        at = base + k * ROWS
        return ref[at : at + ROWS, 0:half], ref[at : at + ROWS, half:PLANE]

    def put(ref, k, val, base=0):
        at = base + k * ROWS
        ref[at : at + ROWS, 0:half] = val[0]
        ref[at : at + ROWS, half:PLANE] = val[1]

    spec[...] = dot_three(moved[...], tab[0], tab[1])
    done = line_transform([piece(spec, k) for k in range(VG)])
    for k in range(VG):
        put(modes, k, done[k])

    def filtered(index, target, base):
        def weighed(k):
            near, far = filters[index, k, 0], filters[index, k, 1]
            (re, im), (twin_re, twin_im) = piece(modes, k), piece(modes, -k % VG)
            return im * near - far * twin_im, re * near + far * twin_re

        for b in range(4):
            group = four_points([weighed(4 * a + b) for a in range(4)])
            for k in range(4):
                put(target, 4 * b + k, times_root(*group[k], b * k), base)
        for k in range(4):
            group = four_points([piece(target, 4 * b + k, base) for b in range(4)])
            for m in range(4):
                re, im = group[m]
                put(target, k + 4 * m, (im, re), base)

    def both(p, target):
        filtered(p, target, 0)
        filtered(p + DIRS, target, rows)

    def product(source):
        got = dot_three(source[...], tab[2], tab[3])
        return got[0:rows] * got[rows:]

    filtered(2 * DIRS, second, 0)
    both(0, first)
    loss = dot_three(second[0:rows, :], tab[2], tab[3])
    gain[...] = -(moved[...] * loss)

    @pl.loop(0, DIRS // 2 - 1)
    def _(h):
        both(2 * h + 1, second)
        gain[...] += product(first)
        both(2 * h + 2, first)
        gain[...] += product(second)

    both(DIRS - 1, second)
    gain[...] += product(first)
    gain[...] += product(second)


def step_kernel(
    dist_in, flags_in, alpha_in, beta_in, loss_in, states_in, tab_in, out,
    dist, flags, alpha, beta, loss, states, tab, load_sem,
    pack_in, recv, left1, right1, coll, edge_out, left2, right2, pack_out, back,
    moved, spec, modes, first, second, gain, packed, filters, near, edge, marks,
    in_send, in_recv, out_send, out_recv, halo_send, halo_recv, flag_send, flag_recv, gate_sem, ready_sem,
):
    s, v = lax.axis_index("space"), lax.axis_index("vel")
    total = lax.axis_size("space")
    group, turn = s // TURNS, s % TURNS
    upper = group % 2
    me = turn * PEERS + v

    def mirror(peer):
        return (peer + PEERS // 2) % PEERS

    def block_of(t, peer):
        return (peer + upper * (mirror(peer) - peer)) * TURNS + t

    def peer_at(q):
        return {"space": group * TURNS + q // PEERS, "vel": q % PEERS}

    right = {"space": (s + TURNS) % total, "vel": mirror(v)}
    left = {"space": (s + total - TURNS) % total, "vel": mirror(v)}
    mine = block_of(turn, v)

    loads = [
        pltpu.make_async_copy(src, dst, load_sem.at[i])
        for i, (src, dst) in enumerate(
            [(flags_in, flags), (alpha_in, alpha), (beta_in, beta), (loss_in, loss), (states_in, states), (tab_in, tab)]
        )
    ]
    quarters = []
    for part in range(4):
        at = pl.ds(part * 32, 32)
        quarters.append(pltpu.make_async_copy(dist_in.at[:, at, :], dist.at[:, at, :], load_sem.at[6 + part]))
        quarters[part].start()
    barrier = pltpu.get_barrier_semaphore()

    @pl.loop(1, GROUP)
    def _(d):
        pl.semaphore_signal(barrier, inc=1, device_id=peer_at((me + d) % GROUP), device_id_type=MESH)

    gate = jnp.logical_and(turn == GATE_TURN, v == GATE_PEER)

    def next_gate(semaphore):
        for step in (TURNS, total - TURNS):
            at = {"space": (s + step) % total, "vel": v}
            pl.semaphore_signal(semaphore, inc=1, device_id=at, device_id_type=MESH)

    @pl.when(gate)
    def _():
        next_gate(barrier)

    for copy in loads:
        copy.start()

    def pack_block(b):
        at = pl.ds(pl.multiple_of(b * ROWS, ROWS), ROWS)
        turned = turn_groups([dist[x, at, part * PLANE : (part + 1) * PLANE] for part in range(2) for x in range(2)])
        for j in range(4):
            pack_in[j % 2, 2 * b + j // 2] = turned[j]

    for part in range(4):
        quarters[part].wait()
        pl.loop(4 * part, 4 * part + 4)(pack_block)

    loads[0].wait()
    pl.semaphore_wait(barrier, jnp.where(gate, GROUP + 1, GROUP - 1))

    def remote(src, dst, send, rec, at):
        return pltpu.make_async_remote_copy(
            src_ref=src, dst_ref=dst, send_sem=send, recv_sem=rec, device_id=at, device_id_type=MESH
        )

    for d in range(1, TURNS):
        at = {"space": group * TURNS + (turn + d) % TURNS, "vel": v}
        remote(flags, near.at[turn], flag_send.at[0], flag_recv.at[0], at).start()
    pltpu.make_async_copy(flags, near.at[turn], flag_recv.at[0]).start()

    upward = jnp.logical_and(turn == TURNS - 1, v >= PEERS // 2)
    downward = jnp.logical_and(turn == 0, v < PEERS // 2)
    kind = jnp.where(upward, 0, jnp.where(downward, 1, 2))
    for n in range(CHUNKS):

        @pl.loop(1, GROUP)
        def _(d):
            q = (me + d) % GROUP
            src = pack_in.at[n, block_of(q // PEERS, q % PEERS)]
            remote(src, recv.at[n, turn, v], in_send.at[n], in_recv.at[n, kind], peer_at(q)).start()

        pltpu.make_async_copy(pack_in.at[n, mine], recv.at[n, turn, v], in_recv.at[n, kind]).start()

    @pl.when(gate)
    def _():
        next_gate(gate_sem)
        pl.semaphore_wait(gate_sem, 2)

        @pl.loop(1, GROUP)
        def _(d):
            pl.semaphore_signal(ready_sem, inc=1, device_id=peer_at((me + d) % GROUP), device_id_type=MESH)

    for copy in loads[1:]:
        copy.wait()

    def pick(rest):
        got = jnp.zeros(rest.shape, f32)
        for _ in range(3):
            one = rest.astype(bf16)
            rest = rest - one.astype(f32)
            got = got + jnp.dot(one, tab[4], preferred_element_type=f32)
        return got

    def by_line(ref):
        return jnp.concatenate([ref[:, k * PLANE : (k + 1) * PLANE] for k in range(VG)], 0)

    packed[0 : VG * DIRS, :] = pick(by_line(alpha))
    packed[VG * DIRS : 2 * VG * DIRS, :] = pick(by_line(beta))
    packed[2 * VG * DIRS :, :] = pick(by_line(loss))
    for k in range(VG):
        for f in range(FILTERS):
            at = 2 * VG * DIRS + k if f == 2 * DIRS else (f // DIRS) * VG * DIRS + k * DIRS + f % DIRS
            for part in range(2):
                row = packed[at : at + 1, part * 128 : (part + 1) * 128]
                filters[f, k, part] = jnp.broadcast_to(row, (ROWS, 128))

    pltpu.make_async_copy(near, near, flag_recv.at[0]).wait()
    @pl.when(jnp.logical_not(gate))
    def _():
        pl.semaphore_wait(ready_sem, 1)

    edges = [
        remote(near.at[3], edge.at[0], flag_send.at[1], flag_recv.at[1], right),
        remote(near.at[0], edge.at[1], flag_send.at[2], flag_recv.at[2], left),
    ]
    for copy in edges:
        copy.start()
    offset = mine * 4
    for n in range(CHUNKS):
        for at, pair in ((1, (0, 3)), (2, (1, 2))):
            rows = [near[pair[r // 2], r % 2 : r % 2 + 1, :] for r in range(4)]
            marks[n, at] = jnp.broadcast_to(flag_tile(rows, offset + 2 * n), (ROWS, PLANE))

    def settle(copies):
        for copy in copies:
            copy.wait()

    def exchange(at, ends, before):
        copies = []
        for way, (src, dst, to) in enumerate(ends):
            before(way, src)
            copies.append(remote(src, dst, halo_send.at[at, way], halo_recv.at[at, way], to))
            copies[way].start()
        return copies

    def begin(n):
        def landed(way, src):
            pltpu.make_async_copy(src, src, in_recv.at[n, way]).wait()

        ends = ((recv.at[n, 3, 4:8], left1.at[n], right), (recv.at[n, 0, 0:4], right1.at[n], left))
        return exchange(n, ends, landed)

    def pass_on(n):
        ends = ((edge_out.at[n, 0], left2.at[n], right), (edge_out.at[n, 1], right2.at[n], left))
        return exchange(CHUNKS + n, ends, lambda way, src: None)

    def rest_of(n):
        rest = recv.at[n, 0:3]
        pltpu.make_async_copy(rest, rest, in_recv.at[n, 2]).wait()

    def work(n, which):
        def tiles_of(u):
            one = swap_halves(recv[n, 0, u], recv[n, 3, u])
            two = swap_halves(recv[n, 1, u], recv[n, 2, u])
            return [(one[part], two[part]) for part in range(2)]

        def halo_of(u, positive):
            return left1[n, u - 4] if positive else right1[n, u]

        def put_moved(u, positive, outs):
            for part in range(2):
                at = pl.multiple_of((2 * u + part) * ROWS, ROWS)
                moved[pl.ds(at, ROWS), :] = outs[part][which]

        transport(lambda r: marks[n, r], states, tiles_of, halo_of, put_moved, which == 0, which == 1)
        collide(filters, tab, moved, spec, modes, first, second, gain)
        for u in range(PEERS):
            pair = []
            for part in range(2):
                at = (2 * u + part) * ROWS
                pair.append(moved[at : at + ROWS, :] + 0.5 * gain[at : at + ROWS, :])
                coll[n, u, part, which] = pair[part]
            if which == 0 and u < 4:
                edge_out[n, 1, u] = swap_halves(*pair)[0]
            if which == 0 and u >= 4:
                edge_out[n, 0, u - 4] = swap_halves(*pair)[1]

    def give(n, t, u):
        q = t * PEERS + u

        @pl.when(q != me)
        def _():
            remote(pack_out.at[n, t, u], back.at[n, mine], out_send.at[n], out_recv.at[n], peer_at(q)).start()

        @pl.when(q == me)
        def _():
            pltpu.make_async_copy(pack_out.at[n, t, u], back.at[n, mine], out_recv.at[n]).start()

    def finish_mid(n):
        def tiles_of(u):
            return [(coll[n, u, part, 1], coll[n, u, part, 1]) for part in range(2)]

        def put_done(u, positive, outs):
            one, two = swap_halves(outs[0][1], outs[1][1])
            if positive:
                pack_out[n, 2, u] = two
            else:
                pack_out[n, 1, u] = one

        transport(lambda r: marks[n, r], states, tiles_of, None, put_done, False, True)

        @pl.loop(0, PEERS)
        def _(d):
            u = (v + 1 + d) % PEERS
            give(n, 1 + u // 4, u)

    def tiles_done(n):
        def tiles_of(u):
            return [(coll[n, u, part, 0], coll[n, u, part, 1]) for part in range(2)]

        return tiles_of

    def finish_most(n):
        def put_done(u, positive, outs):
            one, two = swap_halves(outs[0][1], outs[1][1])
            ends = swap_halves(outs[0][0], outs[1][0])
            if positive:
                pack_out[n, 1, u] = one
                pack_out[n, 3, u] = ends[1]
            else:
                pack_out[n, 2, u] = two
                pack_out[n, 0, u] = ends[0]

        transport(lambda r: marks[n, r], states, tiles_done(n), None, put_done, True, True)

        @pl.loop(0, 2 * PEERS)
        def _(d):
            u = (v + 1 + d) % PEERS
            k = (turn + d // PEERS) % 2
            give(n, (2 - u // 4) * k + (3 * (u // 4)) * (1 - k), u)

    def finish_rest(n):
        def halo_of(u, positive):
            return left2[n, u - 4] if positive else right2[n, u]

        def put_done(u, positive, outs):
            ends = swap_halves(outs[0][0], outs[1][0])
            if positive:
                pack_out[n, 0, u] = ends[0]
            else:
                pack_out[n, 3, u] = ends[1]

        transport(lambda r: marks[n, r], states, tiles_done(n), halo_of, put_done, True, False)

        @pl.loop(0, PEERS)
        def _(d):
            u = (v + 1 + d) % PEERS
            give(n, 3 - 3 * (u // 4), u)

    one1 = begin(0)
    rest_of(0)
    work(0, 1)
    finish_mid(0)
    settle(edges)
    for n in range(CHUNKS):
        lefts = flag_tile([edge[0, 0:1, :], edge[0, 1:2, :], None, None], offset + 2 * n)
        rights = flag_tile([None, None, edge[1, 0:1, :], edge[1, 1:2, :]], offset + 2 * n)
        marks[n, 0] = jnp.broadcast_to(jnp.where(group == 0, 4.0, lefts), (ROWS, PLANE))
        marks[n, 3] = jnp.broadcast_to(jnp.where(group == total // TURNS - 1, 4.0, rights), (ROWS, PLANE))
    two1 = begin(1)
    rest_of(1)
    work(1, 1)
    finish_mid(1)
    settle(one1)
    work(0, 0)
    one2 = pass_on(0)
    finish_most(0)
    settle(two1)
    work(1, 0)
    two2 = pass_on(1)
    finish_most(1)
    settle(one2)
    finish_rest(0)
    settle(two2)
    finish_rest(1)
    for n in range(CHUNKS):
        pltpu.make_async_copy(back.at[n], back.at[n], out_recv.at[n]).wait()

    @pl.loop(0, GROUP // 2)
    def _(b):
        at = pl.ds(pl.multiple_of(b * ROWS, ROWS), ROWS)
        turned = turn_groups([back[j % 2, 2 * b + j // 2] for j in range(4)])
        for part in range(2):
            for x in range(2):
                out[x, at, part * PLANE : (part + 1) * PLANE] = turned[2 * part + x]

    for n in range(CHUNKS):
        for buf, sem in ((pack_in, in_send), (back, out_send)):
            pltpu.make_async_copy(buf.at[n, 0 : GROUP - 1], buf.at[n, 0 : GROUP - 1], sem.at[n]).wait()
    pltpu.make_async_copy(near.at[0:3], near.at[0:3], flag_send.at[0]).wait()


def build(distribution, cell_flags, kernel_alpha, kernel_beta, kernel_loss, boundary_states):
    tile = (ROWS, PLANE)
    block = (VG * ROWS, PLANE)
    double = (2 * VG * ROWS, PLANE)
    anywhere = pl.BlockSpec(memory_space=pl.ANY)
    dma = pltpu.SemaphoreType.DMA

    def room(*dims):
        return pltpu.VMEM(dims + tile, f32)

    return pl.pallas_call(
        step_kernel,
        out_shape=jax.ShapeDtypeStruct(distribution.shape, f32),
        in_specs=[anywhere] * 7,
        out_specs=pl.BlockSpec(memory_space=pltpu.VMEM),
        scratch_shapes=[
            pltpu.VMEM(distribution.shape, f32),
            pltpu.VMEM((2, 128), jnp.int32),
            pltpu.VMEM((DIRS, VEL), f32),
            pltpu.VMEM((DIRS, VEL), f32),
            pltpu.VMEM((1, VEL), f32),
            pltpu.VMEM((2, VEL), f32),
            pltpu.VMEM((5, PLANE, PLANE), bf16),
            dma((10,)),
            room(CHUNKS, GROUP),
            room(CHUNKS, TURNS, PEERS),
            room(CHUNKS, PEERS // 2),
            room(CHUNKS, PEERS // 2),
            room(CHUNKS, PEERS, 2, 2),
            room(CHUNKS, 2, PEERS // 2),
            room(CHUNKS, PEERS // 2),
            room(CHUNKS, PEERS // 2),
            room(CHUNKS, TURNS, PEERS),
            room(CHUNKS, GROUP),
        ]
        + [pltpu.VMEM(block, f32)] * 3
        + [pltpu.VMEM(double, f32)] * 2
        + [pltpu.VMEM(block, f32)]
        + [
            pltpu.VMEM((FILTERS * VG, PLANE), f32),
            pltpu.VMEM((FILTERS, VG, 2, ROWS, 128), f32),
            pltpu.VMEM((TURNS, 2, 128), jnp.int32),
            pltpu.VMEM((2, 2, 128), jnp.int32),
            room(CHUNKS, 4),
            dma((CHUNKS,)),
            dma((CHUNKS, 3)),
            dma((CHUNKS,)),
            dma((CHUNKS,)),
            dma((2 * CHUNKS, 2)),
            dma((2 * CHUNKS, 2)),
            dma((3,)),
            dma((3,)),
            pltpu.SemaphoreType.REGULAR,
            pltpu.SemaphoreType.REGULAR,
        ],
        compiler_params=pltpu.CompilerParams(collective_id=0, has_side_effects=True),
    )(distribution, cell_flags, kernel_alpha, kernel_beta, kernel_loss.reshape(1, VEL), boundary_states, jnp.asarray(tables()))


def solution(mesh):
    return jax.shard_map(
        build,
        mesh=mesh,
        in_specs=(P("space", None, "vel"), P("space", None), P(), P(), P(), P()),
        out_specs=P("space", None, "vel"),
        check_vma=False,
    )
```
